32 devices in a mesh: row: 8 (over z, x), col: 4 (over y, core).
Axes of the slice: x: 2, y: 2, z: 4, core: 2. Of those that a mesh axis runs over, the one named last changes fastest.
Arguments:
- tokens: bfloat16 [3072, 2048], P('row'), may hold values from -6 to 6
- doc_ids: int32 [8, 384], P('row'), may hold values from 0 to 7, never falling along the last dimension, each value on 1 to 192 neighbouring positions
- routes: int32 [3072, 8], P('row'), may hold values from 0 to 127, all different within a row; in each aligned block of 384 rows (0 to 383, 384 to 767, ...) at most 36 rows name the same one
- attn_gain: float32 [2048], replicated, may hold values from 0.25 to 1.75
- w_query: bfloat16 [2048, 4096], P('row', 'col'), may hold values from -0.125 to 0.125
- key_weight: bfloat16 [2048, 512], P('row', 'col'), may hold values from -0.125 to 0.125
- value_weight: bfloat16 [2048, 512], P('row', 'col'), may hold values from -0.125 to 0.125
- w_out: bfloat16 [2048, 4096], P('row', 'col'), may hold values from -0.375 to 0.375
- q_gain: float32 [128], replicated, may hold values from 0.1 to 1.9
- k_gain: float32 [128], replicated, may hold values from 0.1 to 1.9
- ffn_gain: float32 [2048], replicated, may hold values from 0.25 to 1.75
- router: bfloat16 [2048, 128], replicated, may hold values from -0.125 to 0.125
- w_gate: bfloat16 [128, 768, 2048], P('row', 'col'), may hold values from -0.125 to 0.125
- w_up: bfloat16 [128, 768, 2048], P('row', 'col'), may hold values from -0.125 to 0.125
- w_down: bfloat16 [128, 768, 2048], P('row', 'col'), may hold values from -0.4375 to 0.4375
- cotangent: bfloat16 [3072, 2048], P('row'), may hold values from -6 to 6
Outputs:
- block_out: bfloat16 [3072, 2048], P('row')
- grad_tokens: float32 [3072, 2048], P('row')
- grad_attn_gain: float32 [2048], P('row')
- grad_w_query: float32 [2048, 4096], P('row', 'col')
- grad_w_key: float32 [2048, 512], P('row', 'col')
- grad_w_value: float32 [2048, 512], P('row', 'col')
- grad_w_out: float32 [2048, 4096], P('row', 'col')
- grad_q_gain: float32 [128], P('row')
- key_gain_gradient: float32 [128], P('row')
- grad_ffn_gain: float32 [2048], P('row')
- grad_router: float32 [2048, 128], P('row')
- grad_w_gate: float32 [128, 768, 2048], P('row', 'col')
- grad_w_up: float32 [128, 768, 2048], P('row', 'col')
- grad_w_down: float32 [128, 768, 2048], P('row', 'col')
The draws below stay inside these ranges and needn't reach their ends.
Inputs may be any that keep to these rules, and one draw needn't show every extreme that they name: `routes`: each token names 8 different experts. Within one packed sequence (aligned blocks of 384 rows) no expert is named by more than 36 tokens, a bound that some block reaches. `doc_ids`: in each row the document numbers never fall and run through 0 to 7; each document has 1 to 192 tokens, one exactly 192.
All inputs are finite; a program needn't handle non-finite values.
Results may differ from the reference program's by a relative error of at most 0.03.
Values may be sent and summed in bfloat16 or wider, within the bound.
No kernel may reach another device: no remote copies, remote signals or barrier semaphores. Data moves between devices by JAX's collectives and lax.ppermute only.
A program may use at most 512 MiB of HBM per device.

```python
import math
import jax
import jax.numpy as jnp
import numpy as np
from jax import lax

MODEL_WIDTH = 2048
HQ = 32
KEY_VALUE_HEADS = 4
HEAD_SIZE = 128
E = 128
FF = 768
TOPK = 8
TOK_DEV = 384
DOCS = 8
DOC_MOST = 192
CAP = 36
TOKENS = 3072
N_ROW = 8
N_COL = 4


def strengthened(entries, key, source, target, shards_of, factor):
    owner, partner = [(jnp.arange(entries.shape[dim]) // (entries.shape[dim] // shards_of)).reshape([-1 if axis == dim else 1 for axis in range(entries.ndim)]) for dim in (source, target)]
    chosen = jax.random.permutation(key, shards_of)[partner]
    strong = (owner == chosen) | (owner == (partner + shards_of // 2) % shards_of)
    return jnp.where(strong, factor * entries, entries)


def levels(rng, dims, cuts, least, top_value):
    def one(dim, blocks):
        steps = jax.random.uniform(jax.random.fold_in(jax.random.fold_in(rng, 6), dim), (blocks,), jnp.float32, least / len(cuts), top_value / len(cuts))
        return jnp.repeat(jnp.exp(steps), dims[dim] // blocks).reshape((-1,) + (1,) * (len(dims) - dim - 1))

    level = one(*cuts[0])
    for cut in cuts[1:]:
        level = level * one(*cut)
    return level


def profile(count, total, limit, lean):
    weights = [(1 << 20) // math.isqrt(standing ** lean) + 1 for standing in range(2, count + 1)]
    spare, given = total - limit - (count - 1), [1] * (count - 1)
    while spare > 0:
        free = [i for i in range(count - 1) if given[i] < limit]
        pool, remaining = sum([weights[i] for i in free]), spare
        for i in free:
            more = min(limit - given[i], max(1, remaining * weights[i] // pool), spare)
            given[i] = given[i] + more
            spare = spare - more
    return np.array([limit] + given)


def ragged(stream_key, amount, total, limit, lean):
    if amount == 2:
        one = jax.random.randint(stream_key, (), max(1, total - limit), min(limit, total - 1) + 1)
        return jnp.stack([one, total - one])
    tallies = jnp.asarray(profile(amount, total, limit, lean), jnp.int32)
    pairs = (amount - 1) // 2
    donor, receiver = tallies[1:1 + 2 * pairs:2], tallies[2:2 + 2 * pairs:2]
    slack = jnp.minimum(donor - 1, limit - receiver)
    passed = jax.random.randint(jax.random.fold_in(stream_key, 1), (pairs,), 0, 1 << 20) % (slack + 1)
    tallies = tallies.at[1:1 + 2 * pairs:2].set(donor - passed).at[2:2 + 2 * pairs:2].set(receiver + passed)
    return tallies[jax.random.permutation(jax.random.fold_in(stream_key, 2), amount)]


def assign_block(key, own, number, rows, amount, top, bound, slope):
    sequence = jax.random.permutation(key, amount)
    packed, common = load_shares(amount, rows * top, bound, slope, True), load_shares(amount, rows * top, bound, slope, False)
    places = jnp.arange(amount)

    def named(sizes, turn):
        used = int((sizes > 0).sum())
        fixed = max(1, used // 4)
        moved = fixed + (places - fixed + turn * (used - fixed)) % max(1, amount - fixed)
        return jnp.zeros((amount,), jnp.int32).at[sequence[jnp.where(places < fixed, places, moved)]].set(jnp.asarray(sizes, jnp.int32))

    sizes = jnp.where(number % 4 == 0, named(packed, number // 4), named(common, number - number // 4 - 1))
    mixed = jax.random.permutation(jax.random.fold_in(own, 3), amount)
    source_of, taker = mixed[0:amount // 2 * 2:2], mixed[1:amount // 2 * 2:2]
    room = jnp.minimum(sizes[source_of] - 1, bound - sizes[taker]) // 2
    room = jnp.where((source_of == sequence[0]) | (taker == sequence[0]) | (sizes[taker] == 0), 0, jnp.maximum(room, 0))
    moved = jax.random.randint(jax.random.fold_in(own, 4), (amount // 2,), 0, 1 << 20) % (room + 1)
    sizes = sizes.at[source_of].add(-moved).at[taker].add(moved)
    labels = jnp.searchsorted(jnp.cumsum(sizes), jnp.arange(rows * top), side="right").astype(jnp.int32)
    listing = labels.reshape(top, rows).T
    listing = listing[jax.random.permutation(jax.random.fold_in(own, 1), rows)]
    turn = jax.random.randint(jax.random.fold_in(own, 2), (rows, 1), 0, top)
    return jnp.take_along_axis(listing, (jnp.arange(top)[None, :] + turn) % top, axis=1)


def load_shares(number_of, total, most, skew, full):
    loads = [(1 << 20) // math.isqrt(standing ** skew) + 1 for standing in range(1, number_of + 1)]
    largest = most if full else min(most, max(-(-total // number_of), total * loads[0] // sum(loads)))
    least = 1 if total - largest >= number_of - 1 else 0
    given, spare = [largest] + [least] * (number_of - 1), total - largest - least * (number_of - 1)
    while spare > 0:
        free = [i for i in range(1, number_of) if given[i] < largest] or [i for i in range(1, number_of) if given[i] < most]
        mass, remaining = sum([loads[i] for i in free]), spare
        for i in free:
            more = min(most - given[i], max(1, remaining * loads[i] // mass), spare)
            given[i] = given[i] + more
            spare = spare - more
    return np.array(given)


def gaussian(key, dims, scale, limit, pieces=(), held_as=jnp.bfloat16):
    values = jax.random.normal(key, dims, jnp.float32) * scale
    if len(pieces) > 0:
        values = levels(key, dims, pieces, -0.22, 0.18) * values
    return jnp.clip(values, min=-limit, max=limit).astype(held_as)


def gaussian_with(stream_key, extent, spread, bound, pieces, heavy, held_as=jnp.bfloat16):
    entries = spread * jax.random.normal(stream_key, extent, jnp.float32)
    if pieces:
        entries = entries * levels(stream_key, extent, pieces, -0.22, 0.18)
    return jnp.clip(strengthened(entries, jax.random.fold_in(stream_key, 3), *heavy), -bound, bound).astype(held_as)


def setup_inputs(seed: int = 0) -> dict:
    streams_of = jax.random.split(jax.random.key(seed), 17)
    tokens = gaussian(streams_of[0], (TOKENS, MODEL_WIDTH), 1.0, 6.0, ((0, 8),))
    doc_ids = jax.vmap(lambda own: jnp.searchsorted(jnp.cumsum(ragged(own, DOCS, TOK_DEV, DOC_MOST, 2)), jnp.arange(TOK_DEV), side="right"))(jax.random.split(streams_of[1], N_ROW)).reshape((N_ROW, TOK_DEV)).astype(jnp.int32)
    routes_keys = jax.random.split(jax.random.fold_in(streams_of[2], 1), TOKENS // TOK_DEV)
    routes_turns = jax.random.permutation(jax.random.fold_in(streams_of[2], 3), TOKENS // TOK_DEV)
    routes = jax.vmap(lambda own, number: assign_block(jax.random.fold_in(streams_of[2], 2), own, number, TOK_DEV, E, TOPK, CAP, 2))(routes_keys, routes_turns).reshape((TOKENS, TOPK))
    attn_gain = jnp.clip(1.0 + 0.15 * jax.random.normal(streams_of[3], (MODEL_WIDTH,), jnp.float32), 0.25, 1.75)
    w_query = gaussian(streams_of[4], (MODEL_WIDTH, HQ * HEAD_SIZE), MODEL_WIDTH ** -0.5, 0.125, ((0, 8), (1, 4)))
    key_weight = gaussian(streams_of[5], (MODEL_WIDTH, KEY_VALUE_HEADS * HEAD_SIZE), MODEL_WIDTH ** -0.5, 0.125, ((0, 8), (1, 4)))
    value_weight = gaussian(streams_of[6], (MODEL_WIDTH, KEY_VALUE_HEADS * HEAD_SIZE), MODEL_WIDTH ** -0.5, 0.125, ((0, 8), (1, 4)))
    w_out = gaussian(streams_of[7], (MODEL_WIDTH, HQ * HEAD_SIZE), (HQ * HEAD_SIZE // 16) ** -0.5, 0.375, ((0, 8), (1, 4)))
    q_gain = jnp.clip(1.0 + 0.18 * jax.random.normal(streams_of[8], (HEAD_SIZE,), jnp.float32), 0.1, 1.9)
    k_gain = jnp.clip(1.0 + 0.18 * jax.random.normal(streams_of[9], (HEAD_SIZE,), jnp.float32), 0.1, 1.9)
    ffn_gain = jnp.clip(1.0 + 0.15 * jax.random.normal(streams_of[10], (MODEL_WIDTH,), jnp.float32), 0.25, 1.75)
    router = gaussian(streams_of[11], (MODEL_WIDTH, E), MODEL_WIDTH ** -0.5, 0.125)
    w_gate = gaussian(streams_of[12], (E, FF, MODEL_WIDTH), MODEL_WIDTH ** -0.5, 0.125, ((0, 8), (1, 4)))
    w_up = gaussian(streams_of[13], (E, FF, MODEL_WIDTH), MODEL_WIDTH ** -0.5, 0.125, ((0, 8), (1, 4)))
    w_down = gaussian(streams_of[14], (E, FF, MODEL_WIDTH), (FF // 4) ** -0.5, 0.4375, ((0, 8), (1, 4)))
    cotangent = gaussian_with(streams_of[15], (TOKENS, MODEL_WIDTH), 1.0, 6.0, ((0, 8),), (0, 1, 8, 2.0))
    return {"tokens": tokens, "doc_ids": doc_ids, "routes": routes, "attn_gain": attn_gain, "w_query": w_query, "key_weight": key_weight, "value_weight": value_weight, "w_out": w_out, "q_gain": q_gain, "k_gain": k_gain, "ffn_gain": ffn_gain, "router": router, "w_gate": w_gate, "w_up": w_up, "w_down": w_down, "cotangent": cotangent}


epsilon = 1e-06
rope_base = 1000000.0
masked_score = -1e+30

def rms_scale(values, scaling):
    return values * lax.rsqrt(lax.optimization_barrier(jnp.mean(values * values, axis=-1, keepdims=True)) + epsilon) * scaling

def rope_tables(documents):
    length = documents.shape[0]
    earlier = lax.optimization_barrier(jnp.sum((documents[None, :] < documents[:, None]).astype(jnp.int32), axis=1)).astype(jnp.int32)
    position = (jnp.arange(length, dtype=jnp.int32) - earlier).astype(jnp.float32)
    half_width = HEAD_SIZE // 2
    exponent = jnp.arange(half_width, dtype=jnp.float32) * (-2.0 / HEAD_SIZE)
    frequency = jnp.power(jnp.float32(rope_base), exponent)
    angles = position[:, None] * frequency[None, :]
    return (jnp.cos(angles), jnp.sin(angles))

def visible_mask(documents):
    length = documents.shape[0]
    positions_in = jnp.arange(length, dtype=jnp.int32)
    return (documents[:, None] == documents[None, :]) & (positions_in[None, :] <= positions_in[:, None])

def head_prep(raw_heads, scaling, cosine, sine_table):
    normed = rms_scale(raw_heads, scaling)
    half_width = raw_heads.shape[-1] // 2
    front_half = normed[..., :half_width]
    back_half = normed[..., half_width:]
    cos_rows = cosine[:, None, :]
    sin_rows = sine_table[:, None, :]
    return jnp.concatenate([front_half * cos_rows - back_half * sin_rows, back_half * cos_rows + front_half * sin_rows], axis=-1)

def route_gates(logits, chosen_real):
    softmax_all = jax.nn.softmax(logits, axis=-1)
    picked = lax.optimization_barrier(jnp.sum(softmax_all[:, None, :] * chosen_real, axis=-1))
    return picked / lax.optimization_barrier(jnp.sum(picked, axis=-1, keepdims=True))

def attend_forward(queries, key_head_rows, value_heads, visible):
    row_count, head_count, head_width = queries.shape
    group_count = key_head_rows.shape[1]
    grouped = queries.reshape(row_count, group_count, head_count // group_count, head_width).astype(jnp.float32)
    scores = jnp.einsum('tgrh,ugh->grtu', grouped, key_head_rows.astype(jnp.float32)) * head_width ** (-0.5)
    scores = jnp.where(visible[None, None], scores, masked_score)
    row_peak = lax.optimization_barrier(jnp.max(scores, axis=-1, keepdims=True))
    log_norm = row_peak + jnp.log(lax.optimization_barrier(jnp.sum(jnp.exp(scores - row_peak), axis=-1, keepdims=True)))
    attn_weights = jnp.exp(scores - log_norm).astype(jnp.bfloat16)
    context = jnp.einsum('grtu,ugh->tgrh', attn_weights.astype(jnp.float32), value_heads.astype(jnp.float32))
    return (context.reshape(row_count, head_count * head_width).astype(jnp.bfloat16), log_norm)

def attend_backward(queries, key_head_rows, value_heads, visible, log_norm, context, grad_context):
    row_count, head_count, head_width = queries.shape
    group_count = key_head_rows.shape[1]
    repeat = head_count // group_count
    factor = head_width ** (-0.5)
    grouped = queries.reshape(row_count, group_count, repeat, head_width).astype(jnp.float32)
    keys_wide = key_head_rows.astype(jnp.float32)
    values_wide = value_heads.astype(jnp.float32)
    scores = jnp.einsum('tgrh,ugh->grtu', grouped, keys_wide) * factor
    scores = jnp.where(visible[None, None], scores, masked_score)
    weights_wide = jnp.exp(scores - log_norm)
    weights_low = weights_wide.astype(jnp.bfloat16)
    gradient_by_group = grad_context.reshape(row_count, group_count, repeat, head_width).astype(jnp.float32)
    context_by_group = context.reshape(row_count, group_count, repeat, head_width).astype(jnp.float32)
    grad_weights = jnp.einsum('tgrh,ugh->grtu', gradient_by_group, values_wide)
    row_product_sum = jnp.einsum('xjds,xjds->jdx', gradient_by_group, context_by_group)
    grad_scores = (weights_wide * (grad_weights - row_product_sum[..., None]) * factor).astype(jnp.bfloat16)
    grad_queries = jnp.einsum('grtu,ugh->tgrh', grad_scores.astype(jnp.float32), keys_wide)
    key_gradients = jnp.einsum('grtu,tgrh->ugh', grad_scores.astype(jnp.float32), grouped)
    value_gradients = jnp.einsum('grtu,tgrh->ugh', weights_low.astype(jnp.float32), gradient_by_group)
    return (grad_queries.reshape(row_count, head_count, head_width), key_gradients, value_gradients)

def column_parts(active, weight_down):
    row_count = active.shape[0]
    block_width = weight_down.shape[0] // N_COL
    parts = jnp.einsum('rcf,cfd->crd', active.reshape(row_count, N_COL, block_width).astype(jnp.float32), weight_down.reshape(N_COL, block_width, weight_down.shape[1]).astype(jnp.float32))
    return parts.astype(jnp.bfloat16)

def column_back(grad_gate_low, grad_up_low, weight_gate, weight_up):
    row_count = grad_gate_low.shape[0]
    model_width = weight_gate.shape[1]
    block_width = weight_gate.shape[0] // N_COL
    through_gate = jnp.einsum('rcf,cfd->crd', grad_gate_low.reshape(row_count, N_COL, block_width).astype(jnp.float32), weight_gate.reshape(N_COL, block_width, model_width).astype(jnp.float32))
    through_up = jnp.einsum('rcf,cfd->crd', grad_up_low.reshape(row_count, N_COL, block_width).astype(jnp.float32), weight_up.reshape(N_COL, block_width, model_width).astype(jnp.float32))
    return (through_gate + through_up).astype(jnp.bfloat16)

def reference(tokens, doc_ids, routes, attn_gain, w_query, key_weight, value_weight, w_out, q_gain, k_gain, ffn_gain, router, w_gate, w_up, w_down, cotangent):
    token_total = tokens.shape[0]
    count_of_blocks = doc_ids.shape[0]
    rows_each_block = doc_ids.shape[1]
    model_width = tokens.shape[1]
    tokens_wide = tokens.astype(jnp.float32)
    normed_narrow = rms_scale(tokens_wide, attn_gain).astype(jnp.bfloat16)
    query_raw = jnp.dot(normed_narrow, w_query, preferred_element_type=jnp.float32).reshape(token_total, HQ, HEAD_SIZE)
    key_unnormed = jnp.dot(normed_narrow, key_weight, preferred_element_type=jnp.float32).reshape(token_total, KEY_VALUE_HEADS, HEAD_SIZE)
    value_narrow = jnp.dot(normed_narrow, value_weight, preferred_element_type=jnp.float32).astype(jnp.bfloat16).reshape(token_total, KEY_VALUE_HEADS, HEAD_SIZE)
    tables = lax.map(rope_tables, doc_ids)
    cosine = tables[0].reshape(token_total, HEAD_SIZE // 2)
    sine_table = tables[1].reshape(token_total, HEAD_SIZE // 2)
    queries = head_prep(query_raw, q_gain, cosine, sine_table).astype(jnp.bfloat16)
    key_head_rows = head_prep(key_unnormed, k_gain, cosine, sine_table).astype(jnp.bfloat16)
    visible = lax.map(visible_mask, doc_ids)
    query_blocks = queries.reshape(count_of_blocks, rows_each_block, HQ, HEAD_SIZE)
    key_block_list = key_head_rows.reshape(count_of_blocks, rows_each_block, KEY_VALUE_HEADS, HEAD_SIZE)
    value_block_list = value_narrow.reshape(count_of_blocks, rows_each_block, KEY_VALUE_HEADS, HEAD_SIZE)

    def forward_block(element):
        return attend_forward(element[0], element[1], element[2], element[3])
    context_blocks, log_norm = lax.map(forward_block, (query_blocks, key_block_list, value_block_list, visible))
    context = context_blocks.reshape(token_total, HQ * HEAD_SIZE)
    hidden = tokens_wide + jnp.dot(context, w_out.T, preferred_element_type=jnp.float32)
    ffn_low = rms_scale(hidden, ffn_gain).astype(jnp.bfloat16)
    logits = jnp.dot(ffn_low, router, preferred_element_type=jnp.float32)
    chosen = routes[:, :, None] == jnp.arange(E, dtype=jnp.int32)[None, None, :]
    chosen_int = chosen.astype(jnp.int32)
    chosen_real = chosen.astype(jnp.float32)
    gate_weights = route_gates(logits, chosen_real)
    per_token = lax.optimization_barrier(jnp.sum(chosen_int, axis=1)).astype(jnp.int32).reshape(count_of_blocks, rows_each_block, E)
    before = (jnp.cumsum(per_token, axis=1).astype(jnp.int32) - per_token).reshape(token_total, E)
    slot_index = lax.optimization_barrier(jnp.sum(chosen_int * before[:, None, :], axis=-1)).astype(jnp.int32)
    block_index = jnp.arange(token_total, dtype=jnp.int32) // rows_each_block
    flat_index = routes * (count_of_blocks * CAP) + block_index[:, None] * CAP + slot_index
    pair_count = token_total * TOPK
    pair_table = jnp.full((E * count_of_blocks * CAP,), pair_count, jnp.int32).at[flat_index.reshape(-1)].set(jnp.arange(pair_count, dtype=jnp.int32)).reshape(E, count_of_blocks * CAP)
    padded_input = jnp.concatenate([ffn_low, jnp.zeros((1, model_width), jnp.bfloat16)], axis=0)
    padded_gates = jnp.concatenate([gate_weights.reshape(-1), jnp.zeros((1,), jnp.float32)], axis=0)
    grad_out = cotangent.astype(jnp.float32)
    padded_grad = jnp.concatenate([grad_out, jnp.zeros((1, model_width), jnp.float32)], axis=0)

    def expert_forward(mixture, element):
        pairs, weight_gate, weight_up, weight_down = element
        token_rows = pairs // TOPK
        expert_in = padded_input[token_rows]
        gate_pre = jnp.dot(expert_in, weight_gate.T, preferred_element_type=jnp.float32)
        up_pre = jnp.dot(expert_in, weight_up.T, preferred_element_type=jnp.float32)
        active = (gate_pre * jax.nn.sigmoid(gate_pre) * up_pre).astype(jnp.bfloat16)
        parts = column_parts(active, weight_down)
        joined = lax.optimization_barrier(jnp.sum(parts.astype(jnp.float32), axis=0))
        return (mixture.at[token_rows].add(padded_gates[pairs][:, None] * joined), None)
    mixture, unused = lax.scan(expert_forward, jnp.zeros((token_total + 1, model_width), jnp.float32), (pair_table, w_gate, w_up, w_down))
    block_out = (hidden + mixture[:token_total]).astype(jnp.bfloat16)

    def expert_backward(carried, element):
        grad_rows, grad_pairs = carried
        pairs, weight_gate, weight_up, weight_down = element
        token_rows = pairs // TOPK
        expert_in = padded_input[token_rows]
        gate_pre = jnp.dot(expert_in, weight_gate.T, preferred_element_type=jnp.float32)
        up_pre = jnp.dot(expert_in, weight_up.T, preferred_element_type=jnp.float32)
        sigmoid_gate = jax.nn.sigmoid(gate_pre)
        silu_gate = gate_pre * sigmoid_gate
        active = (silu_gate * up_pre).astype(jnp.bfloat16)
        parts = column_parts(active, weight_down)
        grad_selected = padded_grad[token_rows]
        grad_pairs = grad_pairs.at[pairs].add(lax.optimization_barrier(jnp.sum(grad_selected[None] * parts.astype(jnp.float32), axis=(0, 2))))
        grad_expert = (padded_gates[pairs][:, None] * grad_selected).astype(jnp.bfloat16)
        grad_active = jnp.dot(grad_expert, weight_down.T, preferred_element_type=jnp.float32)
        grad_gate_low = (grad_active * up_pre * sigmoid_gate * (1.0 + gate_pre * (1.0 - sigmoid_gate))).astype(jnp.bfloat16)
        grad_up_low = (grad_active * silu_gate).astype(jnp.bfloat16)
        grad_down_here = jnp.dot(active.T, grad_expert, preferred_element_type=jnp.float32)
        grad_gate_here = jnp.dot(grad_gate_low.T, expert_in, preferred_element_type=jnp.float32)
        grad_up_here = jnp.dot(grad_up_low.T, expert_in, preferred_element_type=jnp.float32)
        back_parts = column_back(grad_gate_low, grad_up_low, weight_gate, weight_up)
        grad_rows = grad_rows.at[token_rows].add(lax.optimization_barrier(jnp.sum(back_parts.astype(jnp.float32), axis=0)))
        return ((grad_rows, grad_pairs), (grad_gate_here, grad_up_here, grad_down_here))
    initial = (jnp.zeros((token_total + 1, model_width), jnp.float32), jnp.zeros((pair_count + 1,), jnp.float32))
    (grad_rows, grad_pairs), (grad_w_gate, grad_w_up, grad_w_down) = lax.scan(expert_backward, initial, (pair_table, w_gate, w_up, w_down))
    grad_gates = grad_pairs[:pair_count].reshape(token_total, TOPK)
    unused, gate_pullback = jax.vjp(lambda raw_logits: route_gates(raw_logits, chosen_real), logits)
    grad_logits = gate_pullback(grad_gates)[0].astype(jnp.bfloat16)
    grad_router = jnp.dot(ffn_low.T, grad_logits, preferred_element_type=jnp.float32)
    grad_ffn_normed = grad_rows[:token_total] + jnp.dot(grad_logits, router.T, preferred_element_type=jnp.float32)
    unused, ffn_pullback = jax.vjp(rms_scale, hidden, ffn_gain)
    grad_hidden_norm, grad_ffn_gain = ffn_pullback(grad_ffn_normed)
    grad_hidden = grad_out + grad_hidden_norm
    grad_hidden_low = grad_hidden.astype(jnp.bfloat16)
    grad_w_out = jnp.dot(grad_hidden_low.T, context, preferred_element_type=jnp.float32)
    grad_context = jnp.dot(grad_hidden_low, w_out, preferred_element_type=jnp.float32).astype(jnp.bfloat16)

    def backward_block(element):
        return attend_backward(element[0], element[1], element[2], element[3], element[4], element[5], element[6])
    grad_queries, key_gradients, value_gradients = lax.map(backward_block, (query_blocks, key_block_list, value_block_list, visible, log_norm, context_blocks, grad_context.reshape(count_of_blocks, rows_each_block, HQ * HEAD_SIZE)))
    unused, query_pullback = jax.vjp(lambda raw_heads, scaling: head_prep(raw_heads, scaling, cosine, sine_table), query_raw, q_gain)
    grad_query_raw, grad_q_gain = query_pullback(grad_queries.reshape(token_total, HQ, HEAD_SIZE))
    unused, key_reverse_map = jax.vjp(lambda raw_heads, scaling: head_prep(raw_heads, scaling, cosine, sine_table), key_unnormed, k_gain)
    key_gradient_unnormed, key_gain_gradient = key_reverse_map(key_gradients.reshape(token_total, KEY_VALUE_HEADS, HEAD_SIZE))
    grad_query_low = grad_query_raw.reshape(token_total, HQ * HEAD_SIZE).astype(jnp.bfloat16)
    key_gradient_narrow = key_gradient_unnormed.reshape(token_total, KEY_VALUE_HEADS * HEAD_SIZE).astype(jnp.bfloat16)
    value_gradient_narrow = value_gradients.reshape(token_total, KEY_VALUE_HEADS * HEAD_SIZE).astype(jnp.bfloat16)
    grad_w_query = jnp.dot(normed_narrow.T, grad_query_low, preferred_element_type=jnp.float32)
    grad_w_key = jnp.dot(normed_narrow.T, key_gradient_narrow, preferred_element_type=jnp.float32)
    grad_w_value = jnp.dot(normed_narrow.T, value_gradient_narrow, preferred_element_type=jnp.float32)
    grad_normed = jnp.dot(grad_query_low, w_query.T, preferred_element_type=jnp.float32)
    grad_normed = grad_normed + jnp.dot(key_gradient_narrow, key_weight.T, preferred_element_type=jnp.float32)
    grad_normed = grad_normed + jnp.dot(value_gradient_narrow, value_weight.T, preferred_element_type=jnp.float32)
    unused, attn_pullback = jax.vjp(rms_scale, tokens_wide, attn_gain)
    grad_tokens_norm, grad_attn_gain = attn_pullback(grad_normed)
    grad_tokens = grad_hidden + grad_tokens_norm
    return (block_out, grad_tokens, grad_attn_gain, grad_w_query, grad_w_key, grad_w_value, grad_w_out, grad_q_gain, key_gain_gradient, grad_ffn_gain, grad_router, grad_w_gate, grad_w_up, grad_w_down)
```

```python
import math

import jax
import jax.numpy as jnp
from jax import lax
from jax.experimental import pallas as pl
from jax.experimental.pallas import tpu as pltpu
from jax.sharding import PartitionSpec as P

HEAD_SIZE = 128
TOPK = 8
CAP = 36
CHUNK = 8
SLOTS = -(-CAP // 16) * 16


epsilon = 1e-06
rope_base = 1000000.0
masked_score = -1e30


def rms_scale(values, scaling):
    return values * lax.rsqrt(jnp.mean(values * values, axis=-1, keepdims=True) + epsilon) * scaling


def rope_tables(documents):
    length = documents.shape[0]
    earlier = jnp.sum((documents[None, :] < documents[:, None]).astype(jnp.int32), axis=1)
    position = (jnp.arange(length, dtype=jnp.int32) - earlier).astype(jnp.float32)
    half_width = HEAD_SIZE // 2
    exponent = jnp.arange(half_width, dtype=jnp.float32) * (-2.0 / HEAD_SIZE)
    frequency = jnp.power(jnp.float32(rope_base), exponent)
    angles = position[:, None] * frequency[None, :]
    return (jnp.cos(angles), jnp.sin(angles))


def visible_mask(documents):
    length = documents.shape[0]
    positions_in = jnp.arange(length, dtype=jnp.int32)
    return (documents[:, None] == documents[None, :]) & (
        positions_in[None, :] <= positions_in[:, None]
    )


def head_prep(raw_heads, scaling, cosine, sine_table):
    normed = rms_scale(raw_heads, scaling)
    half_width = raw_heads.shape[-1] // 2
    front_half = normed[..., :half_width]
    back_half = normed[..., half_width:]
    cos_rows = cosine[:, None, :]
    sin_rows = sine_table[:, None, :]
    return jnp.concatenate(
        [
            front_half * cos_rows - back_half * sin_rows,
            back_half * cos_rows + front_half * sin_rows,
        ],
        axis=-1,
    )


def dense_gates(logits, chosen):
    picked = jax.nn.softmax(logits, axis=-1) * chosen
    return picked / jnp.sum(picked, axis=-1, keepdims=True)


def chosen_experts(routes, expert_ids):
    hits = [(routes[:, k : k + 1] == expert_ids[None, :]) for k in range(TOPK)]
    found = hits[0]
    for hit in hits[1:]:
        found = found | hit
    return found


def attend_forward(queries, key_head_rows, value_heads, visible):
    row_count, head_count, head_width = queries.shape
    group_count = key_head_rows.shape[1]
    grouped = queries.reshape(row_count, group_count, head_count // group_count, head_width)
    scores = jnp.einsum(
        "tgrh,ugh->grtu", grouped, key_head_rows, preferred_element_type=jnp.float32
    ) * head_width ** (-0.5)
    scores = jnp.where(visible[None, None], scores, masked_score)
    row_peak = jnp.max(scores, axis=-1, keepdims=True)
    log_norm = row_peak + jnp.log(jnp.sum(jnp.exp(scores - row_peak), axis=-1, keepdims=True))
    attn_weights = jnp.exp(scores - log_norm).astype(jnp.bfloat16)
    context = jnp.einsum(
        "grtu,ugh->tgrh", attn_weights, value_heads, preferred_element_type=jnp.float32
    )
    return (context.reshape(row_count, head_count * head_width).astype(jnp.bfloat16), log_norm)


def attend_backward(queries, key_head_rows, value_heads, visible, log_norm, context, grad_context):
    row_count, head_count, head_width = queries.shape
    group_count = key_head_rows.shape[1]
    repeat = head_count // group_count
    factor = head_width ** (-0.5)
    grouped = queries.reshape(row_count, group_count, repeat, head_width)
    scores = (
        jnp.einsum("tgrh,ugh->grtu", grouped, key_head_rows, preferred_element_type=jnp.float32)
        * factor
    )
    scores = jnp.where(visible[None, None], scores, masked_score)
    weights_wide = jnp.exp(scores - log_norm)
    weights_low = weights_wide.astype(jnp.bfloat16)
    gradient_by_group = grad_context.reshape(row_count, group_count, repeat, head_width)
    context_by_group = context.reshape(row_count, group_count, repeat, head_width)
    grad_weights = jnp.einsum(
        "tgrh,ugh->grtu", gradient_by_group, value_heads, preferred_element_type=jnp.float32
    )
    row_product_sum = jnp.einsum(
        "xjds,xjds->jdx",
        gradient_by_group.astype(jnp.float32),
        context_by_group.astype(jnp.float32),
    )
    grad_scores = (weights_wide * (grad_weights - row_product_sum[..., None]) * factor).astype(
        jnp.bfloat16
    )
    grad_queries = jnp.einsum(
        "grtu,ugh->tgrh", grad_scores, key_head_rows, preferred_element_type=jnp.float32
    )
    key_gradients = jnp.einsum(
        "grtu,tgrh->ugh", grad_scores, grouped, preferred_element_type=jnp.float32
    )
    value_gradients = jnp.einsum(
        "grtu,tgrh->ugh", weights_low, gradient_by_group, preferred_element_type=jnp.float32
    )
    return (grad_queries.reshape(row_count, head_count, head_width), key_gradients, value_gradients)


def ring_order(count):
    evens = list(range(0, count, 2))
    odds = list(range(1, count, 2))
    return evens + odds[::-1]


def ring_links(count):
    order = ring_order(count)
    ahead = [(order[i], order[(i + 1) % count]) for i in range(count)]
    return ahead, [(there, here) for here, there in ahead]


def ring_neighbour(distance):
    count = lax.axis_size("row")
    order = ring_order(count)
    places = [order[(order.index(row) + distance) % count] for row in range(count)]
    return jnp.asarray(places, jnp.int32)[lax.axis_index("row")]


def ring_gather_pieces(shards):
    count = lax.axis_size("row")
    ahead, behind = ring_links(count)
    pieces = [[(lax.axis_index("row"), 0, shard)] for shard in shards]
    forward = backward = list(shards)
    for step in range(1, count // 2):
        forward = [lax.ppermute(piece, "row", ahead) for piece in forward]
        backward = [lax.ppermute(piece, "row", behind) for piece in backward]
        forward, backward = lax.optimization_barrier((forward, backward))
        for found, one, other in zip(pieces, forward, backward):
            found.append((ring_neighbour(-step), 0, one))
            found.append((ring_neighbour(step), 0, other))
    far = ring_neighbour(count // 2)
    for found, one, other in zip(pieces, forward, backward):
        middle = one.shape[0] // 2
        found.append((far, 0, lax.ppermute(one[:middle], "row", ahead)))
        found.append((far, middle, lax.ppermute(other[middle:], "row", behind)))
    return pieces


def assembled(pieces, extent):
    whole = jnp.zeros((lax.axis_size("row") * extent, pieces[0][2].shape[1]), pieces[0][2].dtype)
    for origin, offset, piece in pieces:
        whole = lax.dynamic_update_slice(whole, piece, (origin * extent + offset, 0))
    return whole


def ring_gather(shard):
    return assembled(ring_gather_pieces([shard])[0], shard.shape[0])


def ring_scatter(block_of, wire, fillers=()):
    count = lax.axis_size("row")
    ahead, behind = ring_links(count)
    half = count // 2
    filled = []

    def hop(to_ahead, to_behind):
        step = len(filled)
        to_ahead, to_behind = to_ahead.astype(wire), to_behind.astype(wire)
        filler = fillers[step] if step < len(fillers) else None
        if filler is not None:
            work, operands = filler
            operands = operands(filled) if callable(operands) else operands
            operands, to_ahead, to_behind = lax.optimization_barrier(
                (operands, to_ahead, to_behind)
            )
        forward = lax.ppermute(to_ahead, "row", ahead)
        backward = lax.ppermute(to_behind, "row", behind)
        if filler is not None:
            forward, backward, made = lax.optimization_barrier(
                (forward, backward, work(*operands))
            )
        else:
            forward, backward = lax.optimization_barrier((forward, backward))
            made = None
        filled.append(made)
        return forward.astype(jnp.float32), backward.astype(jnp.float32)

    far = block_of(ring_neighbour(half))
    middle = far.shape[0] // 2
    forward, backward = hop(far[:middle], far[middle:])
    for distance in range(half - 1, -1, -1):
        own_ahead = block_of(ring_neighbour(distance)).astype(jnp.float32)
        own_behind = block_of(ring_neighbour(-distance)).astype(jnp.float32)
        if distance == half - 1:
            to_ahead = jnp.concatenate(
                [own_ahead[:middle] + forward, own_ahead[middle:]], axis=0
            )
            to_behind = jnp.concatenate(
                [own_behind[:middle], own_behind[middle:] + backward], axis=0
            )
        else:
            to_ahead = own_ahead + forward
            to_behind = own_behind + backward
        if distance == 0:
            return to_ahead + backward, filled
        forward, backward = hop(to_ahead, to_behind)


def col_bits():
    count = lax.axis_size("col")
    return [1 << bit for bit in range(count.bit_length() - 1)]


def col_swap(values, bit):
    count = lax.axis_size("col")
    return lax.ppermute(values, "col", [(c, c ^ bit) for c in range(count)])


def split_by_bit(values, bit):
    half = values.shape[0] // 2
    mine = (lax.axis_index("col") // bit) % 2
    keep = lax.dynamic_slice_in_dim(values, mine * half, half, 0)
    give = lax.dynamic_slice_in_dim(values, (1 - mine) * half, half, 0)
    return keep, give


def col_scatter(values):
    count = lax.axis_size("col")
    blocks = values.reshape((count, -1) + values.shape[1:])
    low = blocks.reshape((count // 2, 2) + blocks.shape[1:])
    core = lax.axis_index("col") % 2
    keep = lax.dynamic_index_in_dim(low, core, 1, keepdims=False)
    give = lax.dynamic_index_in_dim(low, 1 - core, 1, keepdims=False)
    total = keep.astype(jnp.float32) + col_swap(give, 1).astype(jnp.float32)
    for bit in reversed(col_bits()[1:]):
        keep, give = split_by_bit(total, bit)
        total = keep + col_swap(give.astype(values.dtype), bit).astype(jnp.float32)
    return total[0]


def col_gather(share):
    count = lax.axis_size("col")
    whole = share[None]
    for bit in reversed(col_bits()):
        other = col_swap(whole, bit)
        mine = (lax.axis_index("col") // bit) % 2
        first = jnp.where(mine == 0, whole, other)
        second = jnp.where(mine == 0, other, whole)
        whole = jnp.stack([first, second], axis=0)
    axes = [len(col_bits()) - 1 - i for i in range(len(col_bits()))]
    whole = whole.reshape((2,) * len(col_bits()) + share.shape)
    whole = whole.transpose(axes + list(range(len(axes), whole.ndim)))
    return whole.reshape((count * share.shape[0],) + share.shape[1:])


def col_sum(values):
    for bit in col_bits():
        values = values + col_swap(values, bit)
    return values


def contract(left, right, left_axis, right_axis):
    return lax.dot_general(
        left,
        right,
        (((left_axis,), (right_axis,)), ((), ())),
        preferred_element_type=jnp.float32,
    )


def whole_block(shape, index_map):
    return pl.BlockSpec(shape, index_map)


def rows_of_slots(match, rows):
    sequences, slot_count, row_count = match.shape
    width = rows.shape[1]

    def kernel(match_ref, rows_ref, out_ref):
        out_ref[0] = contract(match_ref[0], rows_ref[...], 1, 0).astype(out_ref.dtype)

    return pl.pallas_call(
        kernel,
        grid=(sequences,),
        in_specs=[
            whole_block((1, slot_count, row_count), lambda s: (s, 0, 0)),
            whole_block((row_count, width), lambda s: (s, 0)),
        ],
        out_specs=whole_block((1, slot_count, width), lambda s: (s, 0, 0)),
        out_shape=jax.ShapeDtypeStruct((sequences, slot_count, width), rows.dtype),
        name="rows_of_slots",
    )(match, rows)


def gates_of_slots(match, gates):
    sequences, slot_count, row_count = match.shape
    experts = gates.shape[1]

    def kernel(match_ref, gates_ref, out_ref):
        wide = match_ref[0].astype(jnp.float32).reshape(experts, -1, row_count)
        picked = jnp.sum(wide * gates_ref[0][:, None, :], axis=-1, keepdims=True)
        out_ref[0] = picked.reshape(slot_count, 1)

    return pl.pallas_call(
        kernel,
        grid=(sequences,),
        in_specs=[
            whole_block((1, slot_count, row_count), lambda s: (s, 0, 0)),
            whole_block((1, experts, row_count), lambda s: (s, 0, 0)),
        ],
        out_specs=whole_block((1, slot_count, 1), lambda s: (s, 0, 0)),
        out_shape=jax.ShapeDtypeStruct((sequences, slot_count, 1), jnp.float32),
        name="gates_of_slots",
    )(match, gates)


def expert_pass(expert_rows, grad_rows, gate_slots, w_gate, w_up, w_down):
    sequences, experts, slots, width = expert_rows.shape
    hidden_units = w_gate.shape[1]
    chunk = math.gcd(sequences, CHUNK)
    rows = chunk * slots

    def kernel(x_ref, g_ref, gate_ref, wg_ref, wu_ref, wd_ref, out_ref, back_ref, gg_ref, act_ref, dg_ref, du_ref):
        x = x_ref[...].reshape(rows, width)
        gate = gate_ref[...].reshape(rows, 1)
        gate_pre = contract(x, wg_ref[0], 1, 1)
        up_pre = contract(x, wu_ref[0], 1, 1)
        sigmoid_gate = jax.nn.sigmoid(gate_pre)
        silu_gate = gate_pre * sigmoid_gate
        active = (silu_gate * up_pre).astype(jnp.bfloat16)
        act_ref[0] = active
        grad_wide = g_ref[...].reshape(rows, width).astype(jnp.float32)
        grad_expert = (gate * grad_wide).astype(jnp.bfloat16)
        grad_active = contract(grad_expert, wd_ref[0], 1, 1)
        grad_gate_low = (
            grad_active * up_pre * sigmoid_gate * (1.0 + gate_pre * (1.0 - sigmoid_gate))
        ).astype(jnp.bfloat16)
        grad_up_low = (grad_active * silu_gate).astype(jnp.bfloat16)
        dg_ref[0] = grad_gate_low
        du_ref[0] = grad_up_low
        back = contract(grad_gate_low, wg_ref[0], 1, 0) + contract(grad_up_low, wu_ref[0], 1, 0)
        back_ref[...] = back.astype(jnp.bfloat16).reshape(chunk, 1, slots, width)
        expert_out = contract(active, wd_ref[0], 1, 0)
        gg_ref[...] = jnp.sum(expert_out * grad_wide, axis=-1, keepdims=True).reshape(
            chunk, 1, slots, 1
        )
        out_ref[...] = (gate * expert_out).astype(jnp.bfloat16).reshape(chunk, 1, slots, width)

    row_spec = whole_block((chunk, 1, slots, width), lambda e, c: (c, e, 0, 0))
    one_spec = whole_block((chunk, 1, slots, 1), lambda e, c: (c, e, 0, 0))
    weight_spec = whole_block((1, hidden_units, width), lambda e, c: (e, 0, 0))
    hidden_spec = whole_block((1, rows, hidden_units), lambda e, c: (e, c, 0))
    row_shape = jax.ShapeDtypeStruct(expert_rows.shape, jnp.bfloat16)
    hidden_shape = jax.ShapeDtypeStruct((experts, sequences * slots, hidden_units), jnp.bfloat16)
    return pl.pallas_call(
        kernel,
        grid=(experts, sequences // chunk),
        in_specs=[row_spec, row_spec, one_spec, weight_spec, weight_spec, weight_spec],
        out_specs=[row_spec, row_spec, one_spec, hidden_spec, hidden_spec, hidden_spec],
        out_shape=[
            row_shape,
            row_shape,
            jax.ShapeDtypeStruct((sequences, experts, slots, 1), jnp.float32),
            hidden_shape,
            hidden_shape,
            hidden_shape,
        ],
        name="expert_pass",
    )(expert_rows, grad_rows, gate_slots, w_gate, w_up, w_down)


def expert_weight_grads(first, count, operands, earlier):
    sequences, experts, slots, width = operands[0].shape
    hidden_units = operands[3].shape[2]
    chunk = math.gcd(sequences, CHUNK)
    rows = chunk * slots

    def kernel(x_ref, g_ref, gate_ref, act_ref, dg_ref, du_ref, *rest):
        def put(out_ref, left, right):
            term = contract(left, right, 0, 0)
            if sequences == chunk:
                out_ref[0] = term
            else:
                out_ref[0] = term + jnp.where(pl.program_id(1) == 0, 0.0, out_ref[0])

        wg_ref, wu_ref, wd_ref = rest[-3:]
        x = x_ref[...].reshape(rows, width)
        put(wg_ref, dg_ref[0], x)
        put(wu_ref, du_ref[0], x)
        grad_expert = (
            gate_ref[...].reshape(rows, 1) * g_ref[...].reshape(rows, width).astype(jnp.float32)
        ).astype(jnp.bfloat16)
        put(wd_ref, act_ref[0], grad_expert)

    row_spec = whole_block((chunk, 1, slots, width), lambda e, c: (c, first + e, 0, 0))
    one_spec = whole_block((chunk, 1, slots, 1), lambda e, c: (c, first + e, 0, 0))
    weight_spec = whole_block((1, hidden_units, width), lambda e, c: (first + e, 0, 0))
    hidden_spec = whole_block((1, rows, hidden_units), lambda e, c: (first + e, c, 0))
    weight_shape = jax.ShapeDtypeStruct((experts, hidden_units, width), jnp.float32)
    return pl.pallas_call(
        kernel,
        grid=(count, sequences // chunk),
        in_specs=[row_spec, row_spec, one_spec, hidden_spec, hidden_spec, hidden_spec]
        + [pl.BlockSpec(memory_space=pl.ANY)] * len(earlier),
        out_specs=[weight_spec, weight_spec, weight_spec],
        out_shape=[weight_shape, weight_shape, weight_shape],
        input_output_aliases={6 + i: i for i in range(len(earlier))},
        name="expert_weight_grads",
    )(*operands, *earlier)


def slots_to_tokens(match, slot_rows, part, parts):
    sequences, slot_count, row_count = match.shape
    width = slot_rows.shape[2] // parts

    def kernel(part_ref, match_ref, rows_ref, out_ref):
        out_ref[...] = contract(match_ref[0], rows_ref[0], 0, 0).astype(jnp.bfloat16)

    return pl.pallas_call(
        kernel,
        grid_spec=pltpu.PrefetchScalarGridSpec(
            num_scalar_prefetch=1,
            grid=(sequences,),
            in_specs=[
                whole_block((1, slot_count, row_count), lambda s, part: (s, 0, 0)),
                whole_block((1, slot_count, width), lambda s, part: (s, 0, part[0])),
            ],
            out_specs=whole_block((row_count, width), lambda s, part: (s, 0)),
        ),
        out_shape=jax.ShapeDtypeStruct((sequences * row_count, width), jnp.bfloat16),
        name="slots_to_tokens",
    )(part, match, slot_rows)


def gate_grads_to_tokens(match, gate_grads, first_expert, experts_all):
    sequences, slot_count, row_count = match.shape

    def kernel(first_ref, match_ref, gate_ref, out_ref):
        expert_of_slot = first_ref[0] + lax.broadcasted_iota(
            jnp.int32, (slot_count // SLOTS, SLOTS, experts_all), 0
        ).reshape(slot_count, experts_all)
        column = lax.broadcasted_iota(jnp.int32, (slot_count, experts_all), 1)
        placed = jnp.where(column == expert_of_slot, gate_ref[0], 0.0).astype(jnp.bfloat16)
        out_ref[...] = contract(match_ref[0], placed, 0, 0).astype(jnp.bfloat16)

    return pl.pallas_call(
        kernel,
        grid_spec=pltpu.PrefetchScalarGridSpec(
            num_scalar_prefetch=1,
            grid=(sequences,),
            in_specs=[
                whole_block((1, slot_count, row_count), lambda s, first: (s, 0, 0)),
                whole_block((1, slot_count, 1), lambda s, first: (s, 0, 0)),
            ],
            out_specs=whole_block((row_count, experts_all), lambda s, first: (s, 0)),
        ),
        out_shape=jax.ShapeDtypeStruct((sequences * row_count, experts_all), jnp.bfloat16),
        name="gate_grads_to_tokens",
    )(first_expert, match, gate_grads)


def shards(
    tokens,
    doc_ids,
    routes,
    attn_gain,
    w_query,
    key_weight,
    value_weight,
    w_out,
    q_gain,
    k_gain,
    ffn_gain,
    router,
    w_gate,
    w_up,
    w_down,
    cotangent,
):
    row_count, model_width = tokens.shape
    row_devices = lax.axis_size("row")
    col_devices = lax.axis_size("col")
    row_at = lax.axis_index("row")
    col_at = lax.axis_index("col")
    experts_all = router.shape[1]
    local_experts = w_gate.shape[0]
    token_total = row_count * row_devices
    share = row_count // col_devices
    documents = doc_ids[0]
    everyone = ("row", "col")

    def own_share(rows):
        return lax.dynamic_slice_in_dim(rows, col_at * share, share, 0)

    qkv_width = w_query.shape[1] + key_weight.shape[1] + value_weight.shape[1]
    expert_ids = jnp.arange(experts_all, dtype=jnp.int32)
    chosen_row = chosen_experts(routes, expert_ids).astype(jnp.bfloat16)
    chosen_own = own_share(chosen_row)
    qkv_pieces, chosen_pieces = ring_gather_pieces(
        [jnp.concatenate([w_query, key_weight, value_weight], axis=1), chosen_row]
    )
    full_qkv = assembled(qkv_pieces, w_query.shape[0])
    chosen_all = assembled(chosen_pieces, row_count)
    w_out_after, cot_after, unused = lax.optimization_barrier(
        (w_out, own_share(cotangent), qkv_pieces[-4][2])
    )
    full_out = ring_gather(w_out_after)
    cot_all = lax.all_gather(cot_after, everyone, axis=0, tiled=True)
    cosine, sine_table = rope_tables(documents)
    visible = visible_mask(documents)

    first_local = row_at * local_experts
    chosen_local = lax.dynamic_slice_in_dim(chosen_all, first_local, local_experts, 1).reshape(
        row_devices, row_count, local_experts
    )
    positions = jnp.arange(row_count, dtype=jnp.int32)
    earlier = (positions[None, :] < positions[:, None]).astype(jnp.bfloat16)
    rank = jnp.einsum("tu,sue->set", earlier, chosen_local, preferred_element_type=jnp.float32)
    rank = jnp.where(chosen_local.transpose(0, 2, 1) > 0, rank.astype(jnp.int32), SLOTS)
    match = rank[:, :, None, :] == jnp.arange(SLOTS, dtype=jnp.int32)[None, None, :, None]
    slot_total = local_experts * SLOTS
    match = match.astype(jnp.bfloat16).reshape(row_devices, slot_total, row_count)
    slot_shape = (row_devices, local_experts, SLOTS, model_width)
    one_shape = (row_devices, local_experts, SLOTS, 1)
    query_width = w_query.shape[1]
    key_width = key_weight.shape[1]
    tokens_wide = tokens.astype(jnp.float32)
    normed_narrow = rms_scale(tokens_wide, attn_gain).astype(jnp.bfloat16)
    normed_narrow, visible = lax.optimization_barrier((normed_narrow, visible))
    qkv_raw = jnp.dot(normed_narrow, full_qkv, preferred_element_type=jnp.float32)
    query_raw = qkv_raw[:, :query_width].reshape(row_count, -1, HEAD_SIZE)
    key_unnormed = qkv_raw[:, query_width : query_width + key_width].reshape(
        row_count, -1, HEAD_SIZE
    )
    value_narrow = (
        qkv_raw[:, query_width + key_width :]
        .astype(jnp.bfloat16)
        .reshape(row_count, -1, HEAD_SIZE)
    )
    queries = head_prep(query_raw, q_gain, cosine, sine_table).astype(jnp.bfloat16)
    key_head_rows = head_prep(key_unnormed, k_gain, cosine, sine_table).astype(jnp.bfloat16)
    context, log_norm = attend_forward(queries, key_head_rows, value_narrow, visible)
    partial_attn = jnp.einsum("tc,dc->td", context, full_out, preferred_element_type=jnp.float32)
    hidden = own_share(tokens).astype(jnp.float32) + col_scatter(partial_attn.astype(jnp.bfloat16))
    ffn_low = rms_scale(hidden, ffn_gain).astype(jnp.bfloat16)
    ffn_all = lax.all_gather(ffn_low, everyone, axis=0, tiled=True)
    logits = jnp.dot(ffn_low, router, preferred_element_type=jnp.float32)
    gates_all = ring_gather(col_gather(dense_gates(logits, chosen_own.astype(jnp.float32))))
    gates_local = lax.dynamic_slice_in_dim(gates_all, first_local, local_experts, 1)
    gates_local = gates_local.reshape(row_devices, row_count, local_experts).transpose(0, 2, 1)
    gate_slots = gates_of_slots(match, gates_local).reshape(one_shape)
    grad_rows = rows_of_slots(match, cot_all).reshape(slot_shape)
    expert_rows = rows_of_slots(match, ffn_all).reshape(slot_shape)
    gated_out, grad_back, gate_grads, active, grad_gate_low, grad_up_low = expert_pass(
        expert_rows, grad_rows, gate_slots, w_gate, w_up, w_down
    )
    gate_tokens = gate_grads_to_tokens(
        match,
        gate_grads.reshape(row_devices, slot_total, 1),
        first_local.astype(jnp.int32).reshape(1),
        experts_all,
    )
    grad_back, gate_tokens = lax.optimization_barrier((grad_back, gate_tokens))
    grad_back = grad_back.reshape(row_devices, slot_total, model_width)
    gate_sums = lax.psum_scatter(
        gate_tokens, everyone, scatter_dimension=0, tiled=True
    ).astype(jnp.float32)
    core = (col_at % 2).astype(jnp.int32).reshape(1)
    given = slots_to_tokens(match, grad_back, 1 - core, 2)
    taken = col_swap(given, 1)
    kept = slots_to_tokens(match, grad_back, core, 2)

    def pair_block(row):
        mine = lax.dynamic_slice_in_dim(kept, row * row_count, row_count, 0)
        theirs = lax.dynamic_slice_in_dim(taken, row * row_count, row_count, 0)
        return mine.astype(jnp.float32) + theirs.astype(jnp.float32)

    pieces = 4 if local_experts % 4 == 0 else 1
    each = local_experts // pieces
    grad_inputs = (expert_rows, grad_rows, gate_slots, active, grad_gate_low, grad_up_low)

    def weight_grads(piece, earlier):
        return (
            lambda *operands: expert_weight_grads(
                piece * each, each, operands[:6], operands[6:]
            ),
            lambda filled: grad_inputs + tuple(earlier(filled)),
        )

    zero = jnp.zeros((1,), jnp.int32)
    out_filler = (
        lambda *operands: slots_to_tokens(*operands, zero, 1),
        (match, gated_out.reshape(row_devices, slot_total, model_width)),
    )
    weight_fillers = [
        weight_grads(piece, lambda filled, piece=piece: filled[-1 if piece > 1 else 0])
        for piece in range(1, pieces - 1)
    ]
    half_sum, filled = ring_scatter(
        pair_block,
        jnp.bfloat16,
        [weight_grads(0, lambda filled: ()), out_filler] + weight_fillers,
    )
    out_tokens = filled[1]
    weights_so_far = filled[pieces - 1] if pieces > 2 else filled[0]
    for bit in reversed(col_bits()[1:]):
        keep, give = split_by_bit(half_sum, bit)
        half_sum = keep + col_swap(give.astype(jnp.bfloat16), bit).astype(jnp.float32)
    keep, give = split_by_bit(half_sum, 1)
    across = col_swap(give.astype(jnp.bfloat16), 1).astype(jnp.float32)
    back_sum = jnp.where(
        col_at % 2 == 0,
        jnp.concatenate([keep, across], axis=1),
        jnp.concatenate([across, keep], axis=1),
    )
    mixture = lax.psum_scatter(out_tokens, everyone, scatter_dimension=0, tiled=True).astype(
        jnp.float32
    )
    grad_out = own_share(cotangent).astype(jnp.float32)
    unused, gate_pullback = jax.vjp(
        lambda raw_logits: dense_gates(raw_logits, chosen_own.astype(jnp.float32)), logits
    )
    grad_logits = gate_pullback(gate_sums)[0].astype(jnp.bfloat16)
    router_term = jnp.einsum("td,te->ed", ffn_low, grad_logits, preferred_element_type=jnp.float32)
    grad_ffn_normed = back_sum + jnp.einsum(
        "te,de->td", grad_logits, router, preferred_element_type=jnp.float32
    )
    unused, ffn_pullback = jax.vjp(rms_scale, hidden, ffn_gain)
    grad_hidden_norm, ffn_gain_term = ffn_pullback(grad_ffn_normed)
    grad_hidden = grad_out + grad_hidden_norm
    grad_hidden_low = col_gather(grad_hidden.astype(jnp.bfloat16))
    mixture, unused = lax.optimization_barrier((mixture, grad_hidden_low))
    block_out = col_gather((hidden + mixture).astype(jnp.bfloat16))
    out_term = jnp.einsum("td,tc->dc", grad_hidden_low, context, preferred_element_type=jnp.float32)
    out_term = out_term.astype(jnp.bfloat16)

    def block_rows(term):
        extent = model_width // row_devices
        return lambda row: lax.dynamic_slice_in_dim(term, row * extent, extent, 0)

    out_fillers = [
        (
            lambda rows, weights: jnp.einsum(
                "td,dc->tc", rows, weights, preferred_element_type=jnp.float32
            ).astype(jnp.bfloat16),
            (grad_hidden_low, full_out),
        ),
        (
            attend_backward,
            lambda filled: (
                queries, key_head_rows, value_narrow, visible, log_norm, context, filled[0]
            ),
        ),
    ]
    out_sums, filled = ring_scatter(block_rows(out_term), jnp.bfloat16, out_fillers)
    grad_queries, key_gradients, value_gradients = filled[1]
    unused, query_pullback = jax.vjp(
        lambda raw_heads, scaling: head_prep(raw_heads, scaling, cosine, sine_table),
        query_raw,
        q_gain,
    )
    grad_query_raw, q_gain_term = query_pullback(grad_queries)
    unused, key_reverse_map = jax.vjp(
        lambda raw_heads, scaling: head_prep(raw_heads, scaling, cosine, sine_table),
        key_unnormed,
        k_gain,
    )
    key_gradient_unnormed, k_gain_term = key_reverse_map(key_gradients)
    grad_qkv_low = jnp.concatenate(
        [
            grad_query_raw.reshape(row_count, query_width).astype(jnp.bfloat16),
            key_gradient_unnormed.reshape(row_count, key_width).astype(jnp.bfloat16),
            value_gradients.reshape(row_count, key_width).astype(jnp.bfloat16),
        ],
        axis=1,
    )
    qkv_term = jnp.einsum(
        "td,tc->dc", normed_narrow, grad_qkv_low, preferred_element_type=jnp.float32
    )
    partial_grad_normed = jnp.einsum(
        "tc,dc->td", grad_qkv_low, full_qkv, preferred_element_type=jnp.float32
    )
    unused, attn_pullback = jax.vjp(rms_scale, tokens_wide, attn_gain)
    attn_gain_term = attn_pullback(partial_grad_normed)[1]

    last_fillers = (
        [None, weight_grads(pieces - 1, lambda filled: weights_so_far)] if pieces > 1 else []
    )
    qkv_sums, filled = ring_scatter(
        block_rows(qkv_term.astype(jnp.bfloat16)), jnp.bfloat16, last_fillers
    )
    grad_w_gate, grad_w_up, grad_w_down = filled[1] if pieces > 1 else weights_so_far
    extent = model_width // row_devices
    head_share = HEAD_SIZE // row_devices

    def by_rows(gain_term):
        pieces = gain_term.reshape(row_devices, 1, -1)
        return jnp.pad(pieces, ((0, 0), (0, 0), (0, extent - pieces.shape[2])))

    gain_terms = jnp.concatenate(
        [
            by_rows(ffn_gain_term),
            by_rows(attn_gain_term),
            by_rows(q_gain_term),
            by_rows(k_gain_term),
            jnp.zeros((row_devices, 4, extent), jnp.float32),
        ],
        axis=1,
    )
    gain_sums = col_sum(
        ring_scatter(
            lambda row: lax.dynamic_index_in_dim(gain_terms, row, 0, keepdims=False), jnp.float32
        )[0]
    )
    router_blocks = router_term.reshape(experts_all, row_devices, extent).transpose(1, 0, 2)
    router_sums = col_sum(
        ring_scatter(
            lambda row: lax.dynamic_index_in_dim(router_blocks, row, 0, keepdims=False),
            jnp.bfloat16,
        )[0]
    )
    grad_normed = col_gather(
        col_scatter(partial_grad_normed.astype(jnp.bfloat16)).astype(jnp.bfloat16)
    ).astype(jnp.float32)
    grad_tokens = grad_hidden_low.astype(jnp.float32) + attn_pullback(grad_normed)[0]
    grad_w_query = qkv_sums[:, :query_width]
    grad_w_key = qkv_sums[:, query_width : query_width + key_width]
    grad_w_value = qkv_sums[:, query_width + key_width :]
    return (
        block_out,
        grad_tokens,
        gain_sums[1],
        grad_w_query,
        grad_w_key,
        grad_w_value,
        out_sums,
        gain_sums[2, :head_share],
        gain_sums[3, :head_share],
        gain_sums[0],
        router_sums.T,
        grad_w_gate,
        grad_w_up,
        grad_w_down,
    )


def solution(mesh):
    in_specs = (
        P("row", None),
        P("row", None),
        P("row", None),
        P(),
        P("row", "col"),
        P("row", "col"),
        P("row", "col"),
        P("row", "col"),
        P(),
        P(),
        P(),
        P(),
        P("row", "col", None),
        P("row", "col", None),
        P("row", "col", None),
        P("row", None),
    )
    out_specs = (
        P("row", None),
        P("row", None),
        P("row"),
        P("row", "col"),
        P("row", "col"),
        P("row", "col"),
        P("row", "col"),
        P("row"),
        P("row"),
        P("row"),
        P("row", None),
        P("row", "col", None),
        P("row", "col", None),
        P("row", "col", None),
    )
    return jax.shard_map(shards, mesh=mesh, in_specs=in_specs, out_specs=out_specs, check_vma=False)
```

```python
import math

import jax
import jax.numpy as jnp
from jax import lax
from jax.experimental import pallas as pl
from jax.experimental.pallas import tpu as pltpu
from jax.sharding import PartitionSpec as P

HEAD_SIZE = 128
TOPK = 8
CAP = 36
CHUNK = 8
SLOTS = -(-CAP // 16) * 16


epsilon = 1e-06
rope_base = 1000000.0
masked_score = -1e30


def rms_scale(values, scaling):
    return values * lax.rsqrt(jnp.mean(values * values, axis=-1, keepdims=True) + epsilon) * scaling


def rope_tables(documents):
    length = documents.shape[0]
    earlier = jnp.sum((documents[None, :] < documents[:, None]).astype(jnp.int32), axis=1)
    position = (jnp.arange(length, dtype=jnp.int32) - earlier).astype(jnp.float32)
    half_width = HEAD_SIZE // 2
    exponent = jnp.arange(half_width, dtype=jnp.float32) * (-2.0 / HEAD_SIZE)
    frequency = jnp.power(jnp.float32(rope_base), exponent)
    angles = position[:, None] * frequency[None, :]
    return (jnp.cos(angles), jnp.sin(angles))


def visible_mask(documents):
    length = documents.shape[0]
    positions_in = jnp.arange(length, dtype=jnp.int32)
    return (documents[:, None] == documents[None, :]) & (
        positions_in[None, :] <= positions_in[:, None]
    )


def head_prep(raw_heads, scaling, cosine, sine_table):
    normed = rms_scale(raw_heads, scaling)
    half_width = raw_heads.shape[-1] // 2
    front_half = normed[..., :half_width]
    back_half = normed[..., half_width:]
    cos_rows = cosine[:, None, :]
    sin_rows = sine_table[:, None, :]
    return jnp.concatenate(
        [
            front_half * cos_rows - back_half * sin_rows,
            back_half * cos_rows + front_half * sin_rows,
        ],
        axis=-1,
    )


def dense_gates(logits, chosen):
    picked = jax.nn.softmax(logits, axis=-1) * chosen
    return picked / jnp.sum(picked, axis=-1, keepdims=True)


def chosen_experts(routes, expert_ids):
    hits = [(routes[:, k : k + 1] == expert_ids[None, :]) for k in range(TOPK)]
    found = hits[0]
    for hit in hits[1:]:
        found = found | hit
    return found


def attend_forward(queries, key_head_rows, value_heads, visible):
    row_count, head_count, head_width = queries.shape
    group_count = key_head_rows.shape[1]
    grouped = queries.reshape(row_count, group_count, head_count // group_count, head_width)
    scores = jnp.einsum(
        "tgrh,ugh->grtu", grouped, key_head_rows, preferred_element_type=jnp.float32
    ) * head_width ** (-0.5)
    scores = jnp.where(visible[None, None], scores, masked_score)
    row_peak = jnp.max(scores, axis=-1, keepdims=True)
    log_norm = row_peak + jnp.log(jnp.sum(jnp.exp(scores - row_peak), axis=-1, keepdims=True))
    attn_weights = jnp.exp(scores - log_norm).astype(jnp.bfloat16)
    context = jnp.einsum(
        "grtu,ugh->tgrh", attn_weights, value_heads, preferred_element_type=jnp.float32
    )
    return (context.reshape(row_count, head_count * head_width).astype(jnp.bfloat16), log_norm)


def attend_backward(queries, key_head_rows, value_heads, visible, log_norm, context, grad_context):
    row_count, head_count, head_width = queries.shape
    group_count = key_head_rows.shape[1]
    repeat = head_count // group_count
    factor = head_width ** (-0.5)
    grouped = queries.reshape(row_count, group_count, repeat, head_width)
    scores = (
        jnp.einsum("tgrh,ugh->grtu", grouped, key_head_rows, preferred_element_type=jnp.float32)
        * factor
    )
    scores = jnp.where(visible[None, None], scores, masked_score)
    weights_wide = jnp.exp(scores - log_norm)
    weights_low = weights_wide.astype(jnp.bfloat16)
    gradient_by_group = grad_context.reshape(row_count, group_count, repeat, head_width)
    context_by_group = context.reshape(row_count, group_count, repeat, head_width)
    grad_weights = jnp.einsum(
        "tgrh,ugh->grtu", gradient_by_group, value_heads, preferred_element_type=jnp.float32
    )
    row_product_sum = jnp.einsum(
        "xjds,xjds->jdx",
        gradient_by_group.astype(jnp.float32),
        context_by_group.astype(jnp.float32),
    )
    grad_scores = (weights_wide * (grad_weights - row_product_sum[..., None]) * factor).astype(
        jnp.bfloat16
    )
    grad_queries = jnp.einsum(
        "grtu,ugh->tgrh", grad_scores, key_head_rows, preferred_element_type=jnp.float32
    )
    key_gradients = jnp.einsum(
        "grtu,tgrh->ugh", grad_scores, grouped, preferred_element_type=jnp.float32
    )
    value_gradients = jnp.einsum(
        "grtu,tgrh->ugh", weights_low, gradient_by_group, preferred_element_type=jnp.float32
    )
    return (grad_queries.reshape(row_count, head_count, head_width), key_gradients, value_gradients)


def ring_order(count):
    evens = list(range(0, count, 2))
    odds = list(range(1, count, 2))
    return evens + odds[::-1]


def ring_links(count):
    order = ring_order(count)
    ahead = [(order[i], order[(i + 1) % count]) for i in range(count)]
    return ahead, [(there, here) for here, there in ahead]


def ring_neighbour(distance):
    count = lax.axis_size("row")
    order = ring_order(count)
    places = [order[(order.index(row) + distance) % count] for row in range(count)]
    return jnp.asarray(places, jnp.int32)[lax.axis_index("row")]


def ring_gather_pieces(shards, alongside=()):
    count = lax.axis_size("row")
    ahead, behind = ring_links(count)
    pieces = [[(lax.axis_index("row"), 0, shard)] for shard in shards]
    forward = backward = list(shards)
    made = list(alongside)
    for step in range(1, count // 2):
        forward = [lax.ppermute(piece, "row", ahead) for piece in forward]
        backward = [lax.ppermute(piece, "row", behind) for piece in backward]
        if step <= len(made):
            forward, backward, made[step - 1] = lax.optimization_barrier(
                (forward, backward, made[step - 1])
            )
        else:
            forward, backward = lax.optimization_barrier((forward, backward))
        for found, one, other in zip(pieces, forward, backward):
            found.append((ring_neighbour(-step), 0, one))
            found.append((ring_neighbour(step), 0, other))
    far = ring_neighbour(count // 2)
    for found, one, other in zip(pieces, forward, backward):
        middle = one.shape[0] // 2
        found.append((far, 0, lax.ppermute(one[:middle], "row", ahead)))
        found.append((far, middle, lax.ppermute(other[middle:], "row", behind)))
    return pieces, made


def assembled(pieces, extent):
    whole = jnp.zeros((lax.axis_size("row") * extent, pieces[0][2].shape[1]), pieces[0][2].dtype)
    for origin, offset, piece in pieces:
        whole = lax.dynamic_update_slice(whole, piece, (origin * extent + offset, 0))
    return whole


def ring_gather(shard):
    return assembled(ring_gather_pieces([shard])[0][0], shard.shape[0])


def ring_scatter(blocks_of, wires, fillers=()):
    count = lax.axis_size("row")
    ahead, behind = ring_links(count)
    half = count // 2
    filled = []
    marks = []

    def wide(arrays):
        return [array.astype(jnp.float32) for array in arrays]

    def hop(to_ahead, to_behind):
        step = len(filled)
        to_ahead = [array.astype(wire) for array, wire in zip(to_ahead, wires)]
        to_behind = [array.astype(wire) for array, wire in zip(to_behind, wires)]
        to_ahead, to_behind = lax.optimization_barrier((to_ahead, to_behind))
        filler = fillers[step] if step < len(fillers) else None
        forward = [lax.ppermute(array, "row", ahead) for array in to_ahead]
        backward = [lax.ppermute(array, "row", behind) for array in to_behind]
        if filler is not None:
            work, operands = filler
            operands = operands(filled) if callable(operands) else operands
            operands, forward[-1], backward[-1] = lax.optimization_barrier(
                (operands, forward[-1], backward[-1])
            )
        marks.append(forward[-1])
        if filler is not None:
            forward, backward, made = lax.optimization_barrier(
                (forward, backward, work(*operands))
            )
        else:
            forward, backward = lax.optimization_barrier((forward, backward))
            made = None
        filled.append(made)
        return wide(forward), wide(backward)

    far = blocks_of(ring_neighbour(half))
    middles = [array.shape[0] // 2 for array in far]
    forward, backward = hop(
        [array[:middle] for array, middle in zip(far, middles)],
        [array[middle:] for array, middle in zip(far, middles)],
    )
    for distance in range(half - 1, -1, -1):
        to_ahead = wide(blocks_of(ring_neighbour(distance)))
        to_behind = wide(blocks_of(ring_neighbour(-distance)))
        if distance == half - 1:
            to_ahead = [
                jnp.concatenate([own[:middle] + came, own[middle:]], axis=0)
                for own, came, middle in zip(to_ahead, forward, middles)
            ]
            to_behind = [
                jnp.concatenate([own[:middle], own[middle:] + came], axis=0)
                for own, came, middle in zip(to_behind, backward, middles)
            ]
        else:
            to_ahead = [own + came for own, came in zip(to_ahead, forward)]
            to_behind = [own + came for own, came in zip(to_behind, backward)]
        if distance == 0:
            return [one + came for one, came in zip(to_ahead, backward)], filled, marks
        forward, backward = hop(to_ahead, to_behind)


def col_bits():
    count = lax.axis_size("col")
    return [1 << bit for bit in range(count.bit_length() - 1)]


def col_swap(values, bit):
    count = lax.axis_size("col")
    return lax.ppermute(values, "col", [(c, c ^ bit) for c in range(count)])


def split_by_bit(values, bit):
    half = values.shape[0] // 2
    mine = (lax.axis_index("col") // bit) % 2
    keep = lax.dynamic_slice_in_dim(values, mine * half, half, 0)
    give = lax.dynamic_slice_in_dim(values, (1 - mine) * half, half, 0)
    return keep, give


def col_scatter(values):
    count = lax.axis_size("col")
    blocks = values.reshape((count, -1) + values.shape[1:])
    low = blocks.reshape((count // 2, 2) + blocks.shape[1:])
    core = lax.axis_index("col") % 2
    keep = lax.dynamic_index_in_dim(low, core, 1, keepdims=False)
    give = lax.dynamic_index_in_dim(low, 1 - core, 1, keepdims=False)
    total = keep.astype(jnp.float32) + col_swap(give, 1).astype(jnp.float32)
    for bit in reversed(col_bits()[1:]):
        keep, give = split_by_bit(total, bit)
        total = keep + col_swap(give.astype(values.dtype), bit).astype(jnp.float32)
    return total[0]


def col_gather(share):
    count = lax.axis_size("col")
    whole = share[None]
    for bit in reversed(col_bits()):
        other = col_swap(whole, bit)
        mine = (lax.axis_index("col") // bit) % 2
        first = jnp.where(mine == 0, whole, other)
        second = jnp.where(mine == 0, other, whole)
        whole = jnp.stack([first, second], axis=0)
    axes = [len(col_bits()) - 1 - i for i in range(len(col_bits()))]
    whole = whole.reshape((2,) * len(col_bits()) + share.shape)
    whole = whole.transpose(axes + list(range(len(axes), whole.ndim)))
    return whole.reshape((count * share.shape[0],) + share.shape[1:])


def col_sum(values):
    for bit in col_bits():
        values = values + col_swap(values, bit)
    return values


def contract(left, right, left_axis, right_axis):
    return lax.dot_general(
        left,
        right,
        (((left_axis,), (right_axis,)), ((), ())),
        preferred_element_type=jnp.float32,
    )


def whole_block(shape, index_map):
    return pl.BlockSpec(shape, index_map)


def rows_of_slots(match, rows):
    sequences, slot_count, row_count = match.shape
    width = rows.shape[1]

    def kernel(match_ref, rows_ref, out_ref):
        out_ref[0] = contract(match_ref[0], rows_ref[...], 1, 0).astype(out_ref.dtype)

    return pl.pallas_call(
        kernel,
        grid=(sequences,),
        in_specs=[
            whole_block((1, slot_count, row_count), lambda s: (s, 0, 0)),
            whole_block((row_count, width), lambda s: (s, 0)),
        ],
        out_specs=whole_block((1, slot_count, width), lambda s: (s, 0, 0)),
        out_shape=jax.ShapeDtypeStruct((sequences, slot_count, width), rows.dtype),
        name="rows_of_slots",
    )(match, rows)


def rows_of_slots_by_halves(match, core, own_half, other_half):
    sequences, slot_count, row_count = match.shape
    width = own_half.shape[1]

    def kernel(core_ref, match_ref, own_ref, other_ref, out_ref):
        own = contract(match_ref[0], own_ref[...], 1, 0).astype(out_ref.dtype)
        other = contract(match_ref[0], other_ref[...], 1, 0).astype(out_ref.dtype)

        @pl.when(core_ref[0] == 0)
        def first():
            out_ref[0, :, :width] = own
            out_ref[0, :, width:] = other

        @pl.when(core_ref[0] != 0)
        def second():
            out_ref[0, :, :width] = other
            out_ref[0, :, width:] = own

    return pl.pallas_call(
        kernel,
        grid_spec=pltpu.PrefetchScalarGridSpec(
            num_scalar_prefetch=1,
            grid=(sequences,),
            in_specs=[
                whole_block((1, slot_count, row_count), lambda s, core: (s, 0, 0)),
                whole_block((row_count, width), lambda s, core: (s, 0)),
                whole_block((row_count, width), lambda s, core: (s, 0)),
            ],
            out_specs=whole_block((1, slot_count, 2 * width), lambda s, core: (s, 0, 0)),
        ),
        out_shape=jax.ShapeDtypeStruct((sequences, slot_count, 2 * width), own_half.dtype),
        name="rows_of_slots_by_halves",
    )(core, match, own_half, other_half)


def gates_of_slots(match, gates):
    sequences, slot_count, row_count = match.shape
    experts = gates.shape[1]

    def kernel(match_ref, gates_ref, out_ref):
        wide = match_ref[0].astype(jnp.float32).reshape(experts, -1, row_count)
        picked = jnp.sum(wide * gates_ref[0][:, None, :], axis=-1, keepdims=True)
        out_ref[0] = picked.reshape(slot_count, 1)

    return pl.pallas_call(
        kernel,
        grid=(sequences,),
        in_specs=[
            whole_block((1, slot_count, row_count), lambda s: (s, 0, 0)),
            whole_block((1, experts, row_count), lambda s: (s, 0, 0)),
        ],
        out_specs=whole_block((1, slot_count, 1), lambda s: (s, 0, 0)),
        out_shape=jax.ShapeDtypeStruct((sequences, slot_count, 1), jnp.float32),
        name="gates_of_slots",
    )(match, gates)


def expert_pass(expert_rows, grad_rows, gate_slots, w_gate, w_up, w_down):
    sequences, experts, slots, width = expert_rows.shape
    hidden_units = w_gate.shape[1]
    chunk = math.gcd(sequences, CHUNK)
    rows = chunk * slots

    def kernel(x_ref, g_ref, gate_ref, wg_ref, wu_ref, wd_ref, out_ref, back_ref, gg_ref, act_ref, dg_ref, du_ref):
        x = x_ref[...].reshape(rows, width)
        gate = gate_ref[...].reshape(rows, 1)
        gate_pre = contract(x, wg_ref[0], 1, 1)
        up_pre = contract(x, wu_ref[0], 1, 1)
        sigmoid_gate = jax.nn.sigmoid(gate_pre)
        silu_gate = gate_pre * sigmoid_gate
        active = (silu_gate * up_pre).astype(jnp.bfloat16)
        act_ref[0] = active
        grad_wide = g_ref[...].reshape(rows, width).astype(jnp.float32)
        grad_expert = (gate * grad_wide).astype(jnp.bfloat16)
        grad_active = contract(grad_expert, wd_ref[0], 1, 1)
        grad_gate_low = (
            grad_active * up_pre * sigmoid_gate * (1.0 + gate_pre * (1.0 - sigmoid_gate))
        ).astype(jnp.bfloat16)
        grad_up_low = (grad_active * silu_gate).astype(jnp.bfloat16)
        dg_ref[0] = grad_gate_low
        du_ref[0] = grad_up_low
        back = contract(grad_gate_low, wg_ref[0], 1, 0) + contract(grad_up_low, wu_ref[0], 1, 0)
        back_ref[...] = back.astype(jnp.bfloat16).reshape(chunk, 1, slots, width)
        expert_out = contract(active, wd_ref[0], 1, 0)
        gg_ref[...] = jnp.sum(expert_out * grad_wide, axis=-1, keepdims=True).reshape(
            chunk, 1, slots, 1
        )
        out_ref[...] = (gate * expert_out).astype(jnp.bfloat16).reshape(chunk, 1, slots, width)

    row_spec = whole_block((chunk, 1, slots, width), lambda e, c: (c, e, 0, 0))
    one_spec = whole_block((chunk, 1, slots, 1), lambda e, c: (c, e, 0, 0))
    weight_spec = whole_block((1, hidden_units, width), lambda e, c: (e, 0, 0))
    hidden_spec = whole_block((1, rows, hidden_units), lambda e, c: (e, c, 0))
    row_shape = jax.ShapeDtypeStruct(expert_rows.shape, jnp.bfloat16)
    hidden_shape = jax.ShapeDtypeStruct((experts, sequences * slots, hidden_units), jnp.bfloat16)
    return pl.pallas_call(
        kernel,
        grid=(experts, sequences // chunk),
        in_specs=[row_spec, row_spec, one_spec, weight_spec, weight_spec, weight_spec],
        out_specs=[row_spec, row_spec, one_spec, hidden_spec, hidden_spec, hidden_spec],
        out_shape=[
            row_shape,
            row_shape,
            jax.ShapeDtypeStruct((sequences, experts, slots, 1), jnp.float32),
            hidden_shape,
            hidden_shape,
            hidden_shape,
        ],
        name="expert_pass",
    )(expert_rows, grad_rows, gate_slots, w_gate, w_up, w_down)


def expert_weight_grads(first, count, operands, earlier):
    sequences, experts, slots, width = operands[0].shape
    hidden_units = operands[3].shape[2]
    chunk = math.gcd(sequences, CHUNK)
    rows = chunk * slots

    def kernel(x_ref, g_ref, gate_ref, act_ref, dg_ref, du_ref, *rest):
        def put(out_ref, left, right):
            term = contract(left, right, 0, 0)
            if sequences == chunk:
                out_ref[0] = term
            else:
                out_ref[0] = term + jnp.where(pl.program_id(1) == 0, 0.0, out_ref[0])

        wg_ref, wu_ref, wd_ref = rest[-3:]
        x = x_ref[...].reshape(rows, width)
        put(wg_ref, dg_ref[0], x)
        put(wu_ref, du_ref[0], x)
        grad_expert = (
            gate_ref[...].reshape(rows, 1) * g_ref[...].reshape(rows, width).astype(jnp.float32)
        ).astype(jnp.bfloat16)
        put(wd_ref, act_ref[0], grad_expert)

    row_spec = whole_block((chunk, 1, slots, width), lambda e, c: (c, first + e, 0, 0))
    one_spec = whole_block((chunk, 1, slots, 1), lambda e, c: (c, first + e, 0, 0))
    weight_spec = whole_block((1, hidden_units, width), lambda e, c: (first + e, 0, 0))
    hidden_spec = whole_block((1, rows, hidden_units), lambda e, c: (first + e, c, 0))
    weight_shape = jax.ShapeDtypeStruct((experts, hidden_units, width), jnp.float32)
    return pl.pallas_call(
        kernel,
        grid=(count, sequences // chunk),
        in_specs=[row_spec, row_spec, one_spec, hidden_spec, hidden_spec, hidden_spec]
        + [pl.BlockSpec(memory_space=pl.ANY)] * len(earlier),
        out_specs=[weight_spec, weight_spec, weight_spec],
        out_shape=[weight_shape, weight_shape, weight_shape],
        input_output_aliases={6 + i: i for i in range(len(earlier))},
        name="expert_weight_grads",
    )(*operands, *earlier)


def slots_to_tokens(match, slot_rows, part, parts):
    sequences, slot_count, row_count = match.shape
    width = slot_rows.shape[2] // parts

    def kernel(part_ref, match_ref, rows_ref, out_ref):
        out_ref[...] = contract(match_ref[0], rows_ref[0], 0, 0).astype(jnp.bfloat16)

    return pl.pallas_call(
        kernel,
        grid_spec=pltpu.PrefetchScalarGridSpec(
            num_scalar_prefetch=1,
            grid=(sequences,),
            in_specs=[
                whole_block((1, slot_count, row_count), lambda s, part: (s, 0, 0)),
                whole_block((1, slot_count, width), lambda s, part: (s, 0, part[0])),
            ],
            out_specs=whole_block((row_count, width), lambda s, part: (s, 0)),
        ),
        out_shape=jax.ShapeDtypeStruct((sequences * row_count, width), jnp.bfloat16),
        name="slots_to_tokens",
    )(part, match, slot_rows)


def gate_grads_to_tokens(match, gate_grads, first_expert, experts_all):
    sequences, slot_count, row_count = match.shape

    def kernel(first_ref, match_ref, gate_ref, out_ref):
        expert_of_slot = first_ref[0] + lax.broadcasted_iota(
            jnp.int32, (slot_count // SLOTS, SLOTS, experts_all), 0
        ).reshape(slot_count, experts_all)
        column = lax.broadcasted_iota(jnp.int32, (slot_count, experts_all), 1)
        placed = jnp.where(column == expert_of_slot, gate_ref[0], 0.0).astype(jnp.bfloat16)
        out_ref[...] = contract(match_ref[0], placed, 0, 0).astype(jnp.bfloat16)

    return pl.pallas_call(
        kernel,
        grid_spec=pltpu.PrefetchScalarGridSpec(
            num_scalar_prefetch=1,
            grid=(sequences,),
            in_specs=[
                whole_block((1, slot_count, row_count), lambda s, first: (s, 0, 0)),
                whole_block((1, slot_count, 1), lambda s, first: (s, 0, 0)),
            ],
            out_specs=whole_block((row_count, experts_all), lambda s, first: (s, 0)),
        ),
        out_shape=jax.ShapeDtypeStruct((sequences * row_count, experts_all), jnp.bfloat16),
        name="gate_grads_to_tokens",
    )(first_expert, match, gate_grads)


def shards(
    tokens,
    doc_ids,
    routes,
    attn_gain,
    w_query,
    key_weight,
    value_weight,
    w_out,
    q_gain,
    k_gain,
    ffn_gain,
    router,
    w_gate,
    w_up,
    w_down,
    cotangent,
):
    row_count, model_width = tokens.shape
    row_devices = lax.axis_size("row")
    col_devices = lax.axis_size("col")
    row_at = lax.axis_index("row")
    col_at = lax.axis_index("col")
    experts_all = router.shape[1]
    local_experts = w_gate.shape[0]
    token_total = row_count * row_devices
    share = row_count // col_devices
    documents = doc_ids[0]
    everyone = ("row", "col")

    def own_share(rows):
        return lax.dynamic_slice_in_dim(rows, col_at * share, share, 0)

    qkv_width = w_query.shape[1] + key_weight.shape[1] + value_weight.shape[1]
    expert_ids = jnp.arange(experts_all, dtype=jnp.int32)
    chosen_row = chosen_experts(routes, expert_ids).astype(jnp.bfloat16)
    chosen_own = own_share(chosen_row)
    tokens_wide = tokens.astype(jnp.float32)
    normed_narrow = rms_scale(tokens_wide, attn_gain).astype(jnp.bfloat16)
    (qkv_pieces, chosen_pieces), made = ring_gather_pieces(
        [jnp.concatenate([w_query, key_weight, value_weight], axis=1), chosen_row],
        [rope_tables(documents), (normed_narrow, visible_mask(documents))],
    )
    (cosine, sine_table), (normed_narrow, visible) = made
    full_qkv = assembled(qkv_pieces, w_query.shape[0])
    chosen_all = assembled(chosen_pieces, row_count)
    w_out_after, unused = lax.optimization_barrier((w_out, qkv_pieces[-4][2]))
    out_pieces = ring_gather_pieces([w_out_after])[0][0]
    full_out = assembled(out_pieces, w_out.shape[0])
    core = (col_at % 2).astype(jnp.int32).reshape(1)
    half_width = model_width // 2
    half_cotangent = lax.dynamic_slice_in_dim(cotangent, (col_at % 2) * half_width, half_width, 1)
    half_cotangent, unused = lax.optimization_barrier((half_cotangent, out_pieces[-4][2]))
    cot_half = ring_gather(half_cotangent)
    cot_other = col_swap(cot_half, 1)

    first_local = row_at * local_experts
    chosen_local = lax.dynamic_slice_in_dim(chosen_all, first_local, local_experts, 1).reshape(
        row_devices, row_count, local_experts
    )
    positions = jnp.arange(row_count, dtype=jnp.int32)
    earlier = (positions[None, :] < positions[:, None]).astype(jnp.bfloat16)
    rank = jnp.einsum("tu,sue->set", earlier, chosen_local, preferred_element_type=jnp.float32)
    rank = jnp.where(chosen_local.transpose(0, 2, 1) > 0, rank.astype(jnp.int32), SLOTS)
    match = rank[:, :, None, :] == jnp.arange(SLOTS, dtype=jnp.int32)[None, None, :, None]
    slot_total = local_experts * SLOTS
    match = match.astype(jnp.bfloat16).reshape(row_devices, slot_total, row_count)
    slot_shape = (row_devices, local_experts, SLOTS, model_width)
    one_shape = (row_devices, local_experts, SLOTS, 1)
    query_width = w_query.shape[1]
    key_width = key_weight.shape[1]
    qkv_raw = jnp.dot(normed_narrow, full_qkv, preferred_element_type=jnp.float32)
    query_raw = qkv_raw[:, :query_width].reshape(row_count, -1, HEAD_SIZE)
    key_unnormed = qkv_raw[:, query_width : query_width + key_width].reshape(
        row_count, -1, HEAD_SIZE
    )
    value_narrow = (
        qkv_raw[:, query_width + key_width :]
        .astype(jnp.bfloat16)
        .reshape(row_count, -1, HEAD_SIZE)
    )
    queries = head_prep(query_raw, q_gain, cosine, sine_table).astype(jnp.bfloat16)
    key_head_rows = head_prep(key_unnormed, k_gain, cosine, sine_table).astype(jnp.bfloat16)
    context, log_norm = attend_forward(queries, key_head_rows, value_narrow, visible)
    partial_attn = jnp.einsum("tc,dc->td", context, full_out, preferred_element_type=jnp.float32)
    hidden = own_share(tokens).astype(jnp.float32) + col_scatter(partial_attn.astype(jnp.bfloat16))
    ffn_low = rms_scale(hidden, ffn_gain).astype(jnp.bfloat16)
    ffn_all = lax.all_gather(ffn_low, everyone, axis=0, tiled=True)
    logits = jnp.dot(ffn_low, router, preferred_element_type=jnp.float32)
    gates_all = ring_gather(col_gather(dense_gates(logits, chosen_own.astype(jnp.float32))))
    gates_local = lax.dynamic_slice_in_dim(gates_all, first_local, local_experts, 1)
    gates_local = gates_local.reshape(row_devices, row_count, local_experts).transpose(0, 2, 1)
    gate_slots = gates_of_slots(match, gates_local).reshape(one_shape)
    grad_rows = rows_of_slots_by_halves(match, core, cot_half, cot_other).reshape(slot_shape)
    expert_rows = rows_of_slots(match, ffn_all).reshape(slot_shape)
    gated_out, grad_back, gate_grads, active, grad_gate_low, grad_up_low = expert_pass(
        expert_rows, grad_rows, gate_slots, w_gate, w_up, w_down
    )
    gate_tokens = gate_grads_to_tokens(
        match,
        gate_grads.reshape(row_devices, slot_total, 1),
        first_local.astype(jnp.int32).reshape(1),
        experts_all,
    )
    grad_back = grad_back.reshape(row_devices, slot_total, model_width)
    given = slots_to_tokens(match, grad_back, 1 - core, 2)
    taken = col_swap(given, 1)
    kept = slots_to_tokens(match, grad_back, core, 2)

    def pair_block(row):
        mine = lax.dynamic_slice_in_dim(kept, row * row_count, row_count, 0)
        theirs = lax.dynamic_slice_in_dim(taken, row * row_count, row_count, 0)
        gate_block = lax.dynamic_slice_in_dim(gate_tokens, row * row_count, row_count, 0)
        return [mine.astype(jnp.float32) + theirs.astype(jnp.float32), gate_block]

    pieces = 4 if local_experts % 4 == 0 else 1
    each = local_experts // pieces
    grad_inputs = (expert_rows, grad_rows, gate_slots, active, grad_gate_low, grad_up_low)

    def weight_grads(piece, earlier):
        return (
            lambda *operands: expert_weight_grads(
                piece * each, each, operands[:6], operands[6:]
            ),
            lambda filled: grad_inputs + tuple(earlier(filled)),
        )

    zero = jnp.zeros((1,), jnp.int32)
    out_filler = (
        lambda *operands: slots_to_tokens(*operands, zero, 1),
        (match, gated_out.reshape(row_devices, slot_total, model_width)),
    )
    weight_fillers = [
        weight_grads(piece, lambda filled, piece=piece: filled[-1 if piece > 1 else 0])
        for piece in range(1, pieces - 1)
    ]
    (half_sum, gate_sum), filled, unused = ring_scatter(
        pair_block,
        [jnp.bfloat16, jnp.bfloat16],
        [weight_grads(0, lambda filled: ()), out_filler] + weight_fillers,
    )
    out_tokens = filled[1]
    weights_so_far = filled[pieces - 1] if pieces > 2 else filled[0]
    for bit in reversed(col_bits()[1:]):
        keep, give = split_by_bit(half_sum, bit)
        half_sum = keep + col_swap(give.astype(jnp.bfloat16), bit).astype(jnp.float32)
    gate_sums = col_scatter(gate_sum.astype(jnp.bfloat16))
    keep, give = split_by_bit(half_sum, 1)
    across = col_swap(give.astype(jnp.bfloat16), 1).astype(jnp.float32)
    back_sum = jnp.where(
        col_at % 2 == 0,
        jnp.concatenate([keep, across], axis=1),
        jnp.concatenate([across, keep], axis=1),
    )
    mixture = lax.psum_scatter(out_tokens, everyone, scatter_dimension=0, tiled=True).astype(
        jnp.float32
    )
    grad_out = own_share(cotangent).astype(jnp.float32)
    unused, gate_pullback = jax.vjp(
        lambda raw_logits: dense_gates(raw_logits, chosen_own.astype(jnp.float32)), logits
    )
    grad_logits = gate_pullback(gate_sums)[0].astype(jnp.bfloat16)
    router_term = jnp.einsum("td,te->ed", ffn_low, grad_logits, preferred_element_type=jnp.float32)
    grad_ffn_normed = back_sum + jnp.einsum(
        "te,de->td", grad_logits, router, preferred_element_type=jnp.float32
    )
    unused, ffn_pullback = jax.vjp(rms_scale, hidden, ffn_gain)
    grad_hidden_norm, ffn_gain_term = ffn_pullback(grad_ffn_normed)
    grad_hidden = grad_out + grad_hidden_norm
    grad_hidden_low = col_gather(grad_hidden.astype(jnp.bfloat16))
    out_term = jnp.einsum("td,tc->dc", grad_hidden_low, context, preferred_element_type=jnp.float32)
    out_term = out_term.astype(jnp.bfloat16)

    extent = model_width // row_devices

    out_fillers = [
        (
            lambda rows, weights: jnp.einsum(
                "td,dc->tc", rows, weights, preferred_element_type=jnp.float32
            ).astype(jnp.bfloat16),
            (grad_hidden_low, full_out),
        ),
        (
            attend_backward,
            lambda filled: (
                queries, key_head_rows, value_narrow, visible, log_norm, context, filled[0]
            ),
        ),
    ]
    router_blocks = router_term.reshape(experts_all, row_devices, extent).transpose(1, 0, 2)
    router_blocks = router_blocks.astype(jnp.bfloat16)

    def out_blocks(row):
        return [
            lax.dynamic_slice_in_dim(out_term, row * extent, extent, 0),
            lax.dynamic_index_in_dim(router_blocks, row, 0, keepdims=False),
        ]

    (out_sums, router_sums), filled, unused = ring_scatter(
        out_blocks, [jnp.bfloat16, jnp.bfloat16], out_fillers
    )
    grad_queries, key_gradients, value_gradients = filled[1]
    unused, query_pullback = jax.vjp(
        lambda raw_heads, scaling: head_prep(raw_heads, scaling, cosine, sine_table),
        query_raw,
        q_gain,
    )
    grad_query_raw, q_gain_term = query_pullback(grad_queries)
    unused, key_reverse_map = jax.vjp(
        lambda raw_heads, scaling: head_prep(raw_heads, scaling, cosine, sine_table),
        key_unnormed,
        k_gain,
    )
    key_gradient_unnormed, k_gain_term = key_reverse_map(key_gradients)
    grad_qkv_low = jnp.concatenate(
        [
            grad_query_raw.reshape(row_count, query_width).astype(jnp.bfloat16),
            key_gradient_unnormed.reshape(row_count, key_width).astype(jnp.bfloat16),
            value_gradients.reshape(row_count, key_width).astype(jnp.bfloat16),
        ],
        axis=1,
    )
    qkv_term = jnp.einsum(
        "td,tc->dc", normed_narrow, grad_qkv_low, preferred_element_type=jnp.float32
    )
    partial_grad_normed = jnp.einsum(
        "tc,dc->td", grad_qkv_low, full_qkv, preferred_element_type=jnp.float32
    )
    unused, attn_pullback = jax.vjp(rms_scale, tokens_wide, attn_gain)
    attn_gain_term = attn_pullback(partial_grad_normed)[1]

    extent = model_width // row_devices
    head_share = HEAD_SIZE // row_devices

    def by_rows(gain_term):
        pieces = gain_term.reshape(row_devices, 1, -1)
        return jnp.pad(pieces, ((0, 0), (0, 0), (0, extent - pieces.shape[2])))

    gain_terms = jnp.concatenate(
        [
            by_rows(ffn_gain_term),
            by_rows(attn_gain_term),
            by_rows(q_gain_term),
            by_rows(k_gain_term),
            jnp.zeros((row_devices, 4, extent), jnp.float32),
        ],
        axis=1,
    )
    qkv_term = qkv_term.astype(jnp.bfloat16)

    def last_blocks(row):
        return [
            lax.dynamic_slice_in_dim(qkv_term, row * extent, extent, 0),
            lax.dynamic_index_in_dim(gain_terms, row, 0, keepdims=False),
        ]

    def finish(low_rows, summed_rows):
        return col_gather((low_rows + summed_rows).astype(jnp.bfloat16))

    last_weights = weight_grads(pieces - 1, lambda filled: weights_so_far)
    (qkv_sums, gain_sums), filled, marks = ring_scatter(
        last_blocks,
        [jnp.bfloat16, jnp.float32],
        [None, None, (finish, (hidden, mixture)), last_weights if pieces > 1 else None],
    )
    grad_w_gate, grad_w_up, grad_w_down = filled[3] if pieces > 1 else weights_so_far
    partial_low, unused = lax.optimization_barrier(
        (partial_grad_normed.astype(jnp.bfloat16), marks[0])
    )
    block_out = filled[2]
    gain_sums = col_sum(gain_sums)
    router_sums = col_sum(router_sums)
    grad_normed = col_gather(
        col_scatter(partial_low).astype(jnp.bfloat16)
    ).astype(jnp.float32)
    grad_tokens = grad_hidden_low.astype(jnp.float32) + attn_pullback(grad_normed)[0]
    grad_w_query = qkv_sums[:, :query_width]
    grad_w_key = qkv_sums[:, query_width : query_width + key_width]
    grad_w_value = qkv_sums[:, query_width + key_width :]
    return (
        block_out,
        grad_tokens,
        gain_sums[1],
        grad_w_query,
        grad_w_key,
        grad_w_value,
        out_sums,
        gain_sums[2, :head_share],
        gain_sums[3, :head_share],
        gain_sums[0],
        router_sums.T,
        grad_w_gate,
        grad_w_up,
        grad_w_down,
    )


def solution(mesh):
    in_specs = (
        P("row", None),
        P("row", None),
        P("row", None),
        P(),
        P("row", "col"),
        P("row", "col"),
        P("row", "col"),
        P("row", "col"),
        P(),
        P(),
        P(),
        P(),
        P("row", "col", None),
        P("row", "col", None),
        P("row", "col", None),
        P("row", None),
    )
    out_specs = (
        P("row", None),
        P("row", None),
        P("row"),
        P("row", "col"),
        P("row", "col"),
        P("row", "col"),
        P("row", "col"),
        P("row"),
        P("row"),
        P("row"),
        P("row", None),
        P("row", "col", None),
        P("row", "col", None),
        P("row", "col", None),
    )
    return jax.shard_map(shards, mesh=mesh, in_specs=in_specs, out_specs=out_specs, check_vma=False)
```

```python
import math

import jax
import jax.numpy as jnp
from jax import lax
from jax.experimental import pallas as pl
from jax.experimental.pallas import tpu as pltpu
from jax.sharding import PartitionSpec as P

HEAD_SIZE = 128
TOPK = 8
CAP = 36
CHUNK = 8
SLOTS = -(-CAP // 16) * 16


epsilon = 1e-06
rope_base = 1000000.0
masked_score = -1e30


def rms_scale(values, scaling):
    return values * lax.rsqrt(jnp.mean(values * values, axis=-1, keepdims=True) + epsilon) * scaling


def rope_tables(documents):
    length = documents.shape[0]
    earlier = jnp.sum((documents[None, :] < documents[:, None]).astype(jnp.int32), axis=1)
    position = (jnp.arange(length, dtype=jnp.int32) - earlier).astype(jnp.float32)
    half_width = HEAD_SIZE // 2
    exponent = jnp.arange(half_width, dtype=jnp.float32) * (-2.0 / HEAD_SIZE)
    frequency = jnp.power(jnp.float32(rope_base), exponent)
    angles = position[:, None] * frequency[None, :]
    return (jnp.cos(angles), jnp.sin(angles))


def visible_mask(documents):
    length = documents.shape[0]
    positions_in = jnp.arange(length, dtype=jnp.int32)
    return (documents[:, None] == documents[None, :]) & (
        positions_in[None, :] <= positions_in[:, None]
    )


def head_prep(raw_heads, scaling, cosine, sine_table):
    normed = rms_scale(raw_heads, scaling)
    half_width = raw_heads.shape[-1] // 2
    front_half = normed[..., :half_width]
    back_half = normed[..., half_width:]
    cos_rows = cosine[:, None, :]
    sin_rows = sine_table[:, None, :]
    return jnp.concatenate(
        [
            front_half * cos_rows - back_half * sin_rows,
            back_half * cos_rows + front_half * sin_rows,
        ],
        axis=-1,
    )


def dense_gates(logits, chosen):
    picked = jax.nn.softmax(logits, axis=-1) * chosen
    return picked / jnp.sum(picked, axis=-1, keepdims=True)


def chosen_experts(routes, expert_ids):
    hits = [(routes[:, k : k + 1] == expert_ids[None, :]) for k in range(TOPK)]
    found = hits[0]
    for hit in hits[1:]:
        found = found | hit
    return found


def attend_forward(queries, key_head_rows, value_heads, visible):
    row_count, head_count, head_width = queries.shape
    group_count = key_head_rows.shape[1]
    grouped = queries.reshape(row_count, group_count, head_count // group_count, head_width)
    scores = jnp.einsum(
        "tgrh,ugh->grtu", grouped, key_head_rows, preferred_element_type=jnp.float32
    ) * head_width ** (-0.5)
    scores = jnp.where(visible[None, None], scores, masked_score)
    row_peak = jnp.max(scores, axis=-1, keepdims=True)
    log_norm = row_peak + jnp.log(jnp.sum(jnp.exp(scores - row_peak), axis=-1, keepdims=True))
    attn_weights = jnp.exp(scores - log_norm).astype(jnp.bfloat16)
    context = jnp.einsum(
        "grtu,ugh->tgrh", attn_weights, value_heads, preferred_element_type=jnp.float32
    )
    return (context.reshape(row_count, head_count * head_width).astype(jnp.bfloat16), log_norm)


def attend_backward(queries, key_head_rows, value_heads, visible, log_norm, context, grad_context):
    row_count, head_count, head_width = queries.shape
    group_count = key_head_rows.shape[1]
    repeat = head_count // group_count
    factor = head_width ** (-0.5)
    grouped = queries.reshape(row_count, group_count, repeat, head_width)
    scores = (
        jnp.einsum("tgrh,ugh->grtu", grouped, key_head_rows, preferred_element_type=jnp.float32)
        * factor
    )
    scores = jnp.where(visible[None, None], scores, masked_score)
    weights_wide = jnp.exp(scores - log_norm)
    weights_low = weights_wide.astype(jnp.bfloat16)
    gradient_by_group = grad_context.reshape(row_count, group_count, repeat, head_width)
    context_by_group = context.reshape(row_count, group_count, repeat, head_width)
    grad_weights = jnp.einsum(
        "tgrh,ugh->grtu", gradient_by_group, value_heads, preferred_element_type=jnp.float32
    )
    row_product_sum = jnp.einsum(
        "xjds,xjds->jdx",
        gradient_by_group.astype(jnp.float32),
        context_by_group.astype(jnp.float32),
    )
    grad_scores = (weights_wide * (grad_weights - row_product_sum[..., None]) * factor).astype(
        jnp.bfloat16
    )
    grad_queries = jnp.einsum(
        "grtu,ugh->tgrh", grad_scores, key_head_rows, preferred_element_type=jnp.float32
    )
    key_gradients = jnp.einsum(
        "grtu,tgrh->ugh", grad_scores, grouped, preferred_element_type=jnp.float32
    )
    value_gradients = jnp.einsum(
        "grtu,tgrh->ugh", weights_low, gradient_by_group, preferred_element_type=jnp.float32
    )
    return (grad_queries.reshape(row_count, head_count, head_width), key_gradients, value_gradients)


def ring_order(count):
    evens = list(range(0, count, 2))
    odds = list(range(1, count, 2))
    return evens + odds[::-1]


def ring_links(count):
    order = ring_order(count)
    ahead = [(order[i], order[(i + 1) % count]) for i in range(count)]
    return ahead, [(there, here) for here, there in ahead]


def ring_neighbour(distance):
    count = lax.axis_size("row")
    order = ring_order(count)
    places = [order[(order.index(row) + distance) % count] for row in range(count)]
    return jnp.asarray(places, jnp.int32)[lax.axis_index("row")]


def ring_gather_pieces(shards, alongside=()):
    count = lax.axis_size("row")
    ahead, behind = ring_links(count)
    pieces = [[(lax.axis_index("row"), 0, shard)] for shard in shards]
    forward = backward = list(shards)
    made = list(alongside)
    for step in range(1, count // 2):
        forward = [lax.ppermute(piece, "row", ahead) for piece in forward]
        backward = [lax.ppermute(piece, "row", behind) for piece in backward]
        if step <= len(made):
            forward, backward, made[step - 1] = lax.optimization_barrier(
                (forward, backward, made[step - 1])
            )
        else:
            forward, backward = lax.optimization_barrier((forward, backward))
        for found, one, other in zip(pieces, forward, backward):
            found.append((ring_neighbour(-step), 0, one))
            found.append((ring_neighbour(step), 0, other))
    far = ring_neighbour(count // 2)
    for found, one, other in zip(pieces, forward, backward):
        middle = one.shape[0] // 2
        found.append((far, 0, lax.ppermute(one[:middle], "row", ahead)))
        found.append((far, middle, lax.ppermute(other[middle:], "row", behind)))
    return pieces, made


def assembled(pieces, extent):
    whole = jnp.zeros((lax.axis_size("row") * extent, pieces[0][2].shape[1]), pieces[0][2].dtype)
    for origin, offset, piece in pieces:
        whole = lax.dynamic_update_slice(whole, piece, (origin * extent + offset, 0))
    return whole


def ring_gather(shard):
    return assembled(ring_gather_pieces([shard])[0][0], shard.shape[0])


def ring_scatter(blocks_of, wires, fillers=()):
    count = lax.axis_size("row")
    ahead, behind = ring_links(count)
    half = count // 2
    filled = []
    marks = []

    def wide(arrays):
        return [array.astype(jnp.float32) for array in arrays]

    def hop(to_ahead, to_behind):
        step = len(filled)
        to_ahead = [array.astype(wire) for array, wire in zip(to_ahead, wires)]
        to_behind = [array.astype(wire) for array, wire in zip(to_behind, wires)]
        filler = fillers[step] if step < len(fillers) else None
        if filler is not None:
            work, operands = filler
            operands = operands(filled) if callable(operands) else operands
            operands, to_ahead, to_behind = lax.optimization_barrier(
                (operands, to_ahead, to_behind)
            )
        forward = [lax.ppermute(array, "row", ahead) for array in to_ahead]
        backward = [lax.ppermute(array, "row", behind) for array in to_behind]
        marks.append(forward[-1])
        if filler is not None:
            forward, backward, made = lax.optimization_barrier(
                (forward, backward, work(*operands))
            )
        else:
            forward, backward = lax.optimization_barrier((forward, backward))
            made = None
        filled.append(made)
        return wide(forward), wide(backward)

    far = blocks_of(ring_neighbour(half))
    middles = [array.shape[0] // 2 for array in far]
    forward, backward = hop(
        [array[:middle] for array, middle in zip(far, middles)],
        [array[middle:] for array, middle in zip(far, middles)],
    )
    for distance in range(half - 1, -1, -1):
        to_ahead = wide(blocks_of(ring_neighbour(distance)))
        to_behind = wide(blocks_of(ring_neighbour(-distance)))
        if distance == half - 1:
            to_ahead = [
                jnp.concatenate([own[:middle] + came, own[middle:]], axis=0)
                for own, came, middle in zip(to_ahead, forward, middles)
            ]
            to_behind = [
                jnp.concatenate([own[:middle], own[middle:] + came], axis=0)
                for own, came, middle in zip(to_behind, backward, middles)
            ]
        else:
            to_ahead = [own + came for own, came in zip(to_ahead, forward)]
            to_behind = [own + came for own, came in zip(to_behind, backward)]
        if distance == 0:
            return [one + came for one, came in zip(to_ahead, backward)], filled, marks
        forward, backward = hop(to_ahead, to_behind)


def col_bits():
    count = lax.axis_size("col")
    return [1 << bit for bit in range(count.bit_length() - 1)]


def col_swap(values, bit):
    count = lax.axis_size("col")
    return lax.ppermute(values, "col", [(c, c ^ bit) for c in range(count)])


def split_by_bit(values, bit):
    half = values.shape[0] // 2
    mine = (lax.axis_index("col") // bit) % 2
    keep = lax.dynamic_slice_in_dim(values, mine * half, half, 0)
    give = lax.dynamic_slice_in_dim(values, (1 - mine) * half, half, 0)
    return keep, give


def col_scatter(values):
    count = lax.axis_size("col")
    blocks = values.reshape((count, -1) + values.shape[1:])
    low = blocks.reshape((count // 2, 2) + blocks.shape[1:])
    core = lax.axis_index("col") % 2
    keep = lax.dynamic_index_in_dim(low, core, 1, keepdims=False)
    give = lax.dynamic_index_in_dim(low, 1 - core, 1, keepdims=False)
    total = keep.astype(jnp.float32) + col_swap(give, 1).astype(jnp.float32)
    for bit in reversed(col_bits()[1:]):
        keep, give = split_by_bit(total, bit)
        total = keep + col_swap(give.astype(values.dtype), bit).astype(jnp.float32)
    return total[0]


def col_gather(share):
    count = lax.axis_size("col")
    whole = share[None]
    for bit in reversed(col_bits()):
        other = col_swap(whole, bit)
        mine = (lax.axis_index("col") // bit) % 2
        first = jnp.where(mine == 0, whole, other)
        second = jnp.where(mine == 0, other, whole)
        whole = jnp.stack([first, second], axis=0)
    axes = [len(col_bits()) - 1 - i for i in range(len(col_bits()))]
    whole = whole.reshape((2,) * len(col_bits()) + share.shape)
    whole = whole.transpose(axes + list(range(len(axes), whole.ndim)))
    return whole.reshape((count * share.shape[0],) + share.shape[1:])


def col_sum(values):
    for bit in col_bits():
        values = values + col_swap(values, bit)
    return values


def contract(left, right, left_axis, right_axis):
    return lax.dot_general(
        left,
        right,
        (((left_axis,), (right_axis,)), ((), ())),
        preferred_element_type=jnp.float32,
    )


def whole_block(shape, index_map):
    return pl.BlockSpec(shape, index_map)


def rows_of_slots(match, rows):
    sequences, slot_count, row_count = match.shape
    width = rows.shape[1]

    def kernel(match_ref, rows_ref, out_ref):
        out_ref[0] = contract(match_ref[0], rows_ref[...], 1, 0).astype(out_ref.dtype)

    return pl.pallas_call(
        kernel,
        grid=(sequences,),
        in_specs=[
            whole_block((1, slot_count, row_count), lambda s: (s, 0, 0)),
            whole_block((row_count, width), lambda s: (s, 0)),
        ],
        out_specs=whole_block((1, slot_count, width), lambda s: (s, 0, 0)),
        out_shape=jax.ShapeDtypeStruct((sequences, slot_count, width), rows.dtype),
        name="rows_of_slots",
    )(match, rows)


def gates_of_slots(match, gates):
    sequences, slot_count, row_count = match.shape
    experts = gates.shape[1]

    def kernel(match_ref, gates_ref, out_ref):
        wide = match_ref[0].astype(jnp.float32).reshape(experts, -1, row_count)
        picked = jnp.sum(wide * gates_ref[0][:, None, :], axis=-1, keepdims=True)
        out_ref[0] = picked.reshape(slot_count, 1)

    return pl.pallas_call(
        kernel,
        grid=(sequences,),
        in_specs=[
            whole_block((1, slot_count, row_count), lambda s: (s, 0, 0)),
            whole_block((1, experts, row_count), lambda s: (s, 0, 0)),
        ],
        out_specs=whole_block((1, slot_count, 1), lambda s: (s, 0, 0)),
        out_shape=jax.ShapeDtypeStruct((sequences, slot_count, 1), jnp.float32),
        name="gates_of_slots",
    )(match, gates)


def expert_pass(expert_rows, grad_rows, gate_slots, w_gate, w_up, w_down):
    sequences, experts, slots, width = expert_rows.shape
    hidden_units = w_gate.shape[1]
    chunk = math.gcd(sequences, CHUNK)
    rows = chunk * slots

    def kernel(x_ref, g_ref, gate_ref, wg_ref, wu_ref, wd_ref, out_ref, back_ref, gg_ref, act_ref, dg_ref, du_ref):
        x = x_ref[...].reshape(rows, width)
        gate = gate_ref[...].reshape(rows, 1)
        gate_pre = contract(x, wg_ref[0], 1, 1)
        up_pre = contract(x, wu_ref[0], 1, 1)
        sigmoid_gate = jax.nn.sigmoid(gate_pre)
        silu_gate = gate_pre * sigmoid_gate
        active = (silu_gate * up_pre).astype(jnp.bfloat16)
        act_ref[0] = active
        grad_wide = g_ref[...].reshape(rows, width).astype(jnp.float32)
        grad_expert = (gate * grad_wide).astype(jnp.bfloat16)
        grad_active = contract(grad_expert, wd_ref[0], 1, 1)
        grad_gate_low = (
            grad_active * up_pre * sigmoid_gate * (1.0 + gate_pre * (1.0 - sigmoid_gate))
        ).astype(jnp.bfloat16)
        grad_up_low = (grad_active * silu_gate).astype(jnp.bfloat16)
        dg_ref[0] = grad_gate_low
        du_ref[0] = grad_up_low
        back = contract(grad_gate_low, wg_ref[0], 1, 0) + contract(grad_up_low, wu_ref[0], 1, 0)
        back_ref[...] = back.astype(jnp.bfloat16).reshape(chunk, 1, slots, width)
        expert_out = contract(active, wd_ref[0], 1, 0)
        gg_ref[...] = jnp.sum(expert_out * grad_wide, axis=-1, keepdims=True).reshape(
            chunk, 1, slots, 1
        )
        out_ref[...] = (gate * expert_out).astype(jnp.bfloat16).reshape(chunk, 1, slots, width)

    row_spec = whole_block((chunk, 1, slots, width), lambda e, c: (c, e, 0, 0))
    one_spec = whole_block((chunk, 1, slots, 1), lambda e, c: (c, e, 0, 0))
    weight_spec = whole_block((1, hidden_units, width), lambda e, c: (e, 0, 0))
    hidden_spec = whole_block((1, rows, hidden_units), lambda e, c: (e, c, 0))
    row_shape = jax.ShapeDtypeStruct(expert_rows.shape, jnp.bfloat16)
    hidden_shape = jax.ShapeDtypeStruct((experts, sequences * slots, hidden_units), jnp.bfloat16)
    return pl.pallas_call(
        kernel,
        grid=(experts, sequences // chunk),
        in_specs=[row_spec, row_spec, one_spec, weight_spec, weight_spec, weight_spec],
        out_specs=[row_spec, row_spec, one_spec, hidden_spec, hidden_spec, hidden_spec],
        out_shape=[
            row_shape,
            row_shape,
            jax.ShapeDtypeStruct((sequences, experts, slots, 1), jnp.float32),
            hidden_shape,
            hidden_shape,
            hidden_shape,
        ],
        name="expert_pass",
    )(expert_rows, grad_rows, gate_slots, w_gate, w_up, w_down)


def expert_weight_grads(first, count, operands, earlier):
    sequences, experts, slots, width = operands[0].shape
    hidden_units = operands[3].shape[2]
    chunk = math.gcd(sequences, CHUNK)
    rows = chunk * slots

    def kernel(x_ref, g_ref, gate_ref, act_ref, dg_ref, du_ref, *rest):
        def put(out_ref, left, right):
            term = contract(left, right, 0, 0)
            if sequences == chunk:
                out_ref[0] = term
            else:
                out_ref[0] = term + jnp.where(pl.program_id(1) == 0, 0.0, out_ref[0])

        wg_ref, wu_ref, wd_ref = rest[-3:]
        x = x_ref[...].reshape(rows, width)
        put(wg_ref, dg_ref[0], x)
        put(wu_ref, du_ref[0], x)
        grad_expert = (
            gate_ref[...].reshape(rows, 1) * g_ref[...].reshape(rows, width).astype(jnp.float32)
        ).astype(jnp.bfloat16)
        put(wd_ref, act_ref[0], grad_expert)

    row_spec = whole_block((chunk, 1, slots, width), lambda e, c: (c, first + e, 0, 0))
    one_spec = whole_block((chunk, 1, slots, 1), lambda e, c: (c, first + e, 0, 0))
    weight_spec = whole_block((1, hidden_units, width), lambda e, c: (first + e, 0, 0))
    hidden_spec = whole_block((1, rows, hidden_units), lambda e, c: (first + e, c, 0))
    weight_shape = jax.ShapeDtypeStruct((experts, hidden_units, width), jnp.float32)
    return pl.pallas_call(
        kernel,
        grid=(count, sequences // chunk),
        in_specs=[row_spec, row_spec, one_spec, hidden_spec, hidden_spec, hidden_spec]
        + [pl.BlockSpec(memory_space=pl.ANY)] * len(earlier),
        out_specs=[weight_spec, weight_spec, weight_spec],
        out_shape=[weight_shape, weight_shape, weight_shape],
        input_output_aliases={6 + i: i for i in range(len(earlier))},
        name="expert_weight_grads",
    )(*operands, *earlier)


def slots_to_tokens(match, slot_rows, part, parts):
    sequences, slot_count, row_count = match.shape
    width = slot_rows.shape[2] // parts

    def kernel(part_ref, match_ref, rows_ref, out_ref):
        out_ref[...] = contract(match_ref[0], rows_ref[0], 0, 0).astype(jnp.bfloat16)

    return pl.pallas_call(
        kernel,
        grid_spec=pltpu.PrefetchScalarGridSpec(
            num_scalar_prefetch=1,
            grid=(sequences,),
            in_specs=[
                whole_block((1, slot_count, row_count), lambda s, part: (s, 0, 0)),
                whole_block((1, slot_count, width), lambda s, part: (s, 0, part[0])),
            ],
            out_specs=whole_block((row_count, width), lambda s, part: (s, 0)),
        ),
        out_shape=jax.ShapeDtypeStruct((sequences * row_count, width), jnp.bfloat16),
        name="slots_to_tokens",
    )(part, match, slot_rows)


def gate_grads_to_tokens(match, gate_grads, first_expert, experts_all):
    sequences, slot_count, row_count = match.shape

    def kernel(first_ref, match_ref, gate_ref, out_ref):
        expert_of_slot = first_ref[0] + lax.broadcasted_iota(
            jnp.int32, (slot_count // SLOTS, SLOTS, experts_all), 0
        ).reshape(slot_count, experts_all)
        column = lax.broadcasted_iota(jnp.int32, (slot_count, experts_all), 1)
        placed = jnp.where(column == expert_of_slot, gate_ref[0], 0.0).astype(jnp.bfloat16)
        out_ref[...] = contract(match_ref[0], placed, 0, 0).astype(jnp.bfloat16)

    return pl.pallas_call(
        kernel,
        grid_spec=pltpu.PrefetchScalarGridSpec(
            num_scalar_prefetch=1,
            grid=(sequences,),
            in_specs=[
                whole_block((1, slot_count, row_count), lambda s, first: (s, 0, 0)),
                whole_block((1, slot_count, 1), lambda s, first: (s, 0, 0)),
            ],
            out_specs=whole_block((row_count, experts_all), lambda s, first: (s, 0)),
        ),
        out_shape=jax.ShapeDtypeStruct((sequences * row_count, experts_all), jnp.bfloat16),
        name="gate_grads_to_tokens",
    )(first_expert, match, gate_grads)


def shards(
    tokens,
    doc_ids,
    routes,
    attn_gain,
    w_query,
    key_weight,
    value_weight,
    w_out,
    q_gain,
    k_gain,
    ffn_gain,
    router,
    w_gate,
    w_up,
    w_down,
    cotangent,
):
    row_count, model_width = tokens.shape
    row_devices = lax.axis_size("row")
    col_devices = lax.axis_size("col")
    row_at = lax.axis_index("row")
    col_at = lax.axis_index("col")
    experts_all = router.shape[1]
    local_experts = w_gate.shape[0]
    token_total = row_count * row_devices
    share = row_count // col_devices
    documents = doc_ids[0]
    everyone = ("row", "col")

    def own_share(rows):
        return lax.dynamic_slice_in_dim(rows, col_at * share, share, 0)

    qkv_width = w_query.shape[1] + key_weight.shape[1] + value_weight.shape[1]
    expert_ids = jnp.arange(experts_all, dtype=jnp.int32)
    chosen_row = chosen_experts(routes, expert_ids).astype(jnp.bfloat16)
    chosen_own = own_share(chosen_row)
    tokens_wide = tokens.astype(jnp.float32)
    normed_narrow = rms_scale(tokens_wide, attn_gain).astype(jnp.bfloat16)
    (qkv_pieces, chosen_pieces), made = ring_gather_pieces(
        [jnp.concatenate([w_query, key_weight, value_weight], axis=1), chosen_row],
        [rope_tables(documents), (normed_narrow, visible_mask(documents))],
    )
    (cosine, sine_table), (normed_narrow, visible) = made
    full_qkv = assembled(qkv_pieces, w_query.shape[0])
    chosen_all = assembled(chosen_pieces, row_count)
    w_out_after, unused = lax.optimization_barrier((w_out, qkv_pieces[-4][2]))
    out_pieces = ring_gather_pieces([w_out_after])[0][0]
    full_out = assembled(out_pieces, w_out.shape[0])
    core = (col_at % 2).astype(jnp.int32).reshape(1)
    cot_share, unused = lax.optimization_barrier((own_share(cotangent), out_pieces[-4][2]))
    cot_all = lax.all_gather(cot_share, everyone, axis=0, tiled=True)

    first_local = row_at * local_experts
    chosen_local = lax.dynamic_slice_in_dim(chosen_all, first_local, local_experts, 1).reshape(
        row_devices, row_count, local_experts
    )
    positions = jnp.arange(row_count, dtype=jnp.int32)
    earlier = (positions[None, :] < positions[:, None]).astype(jnp.bfloat16)
    rank = jnp.einsum("tu,sue->set", earlier, chosen_local, preferred_element_type=jnp.float32)
    rank = jnp.where(chosen_local.transpose(0, 2, 1) > 0, rank.astype(jnp.int32), SLOTS)
    match = rank[:, :, None, :] == jnp.arange(SLOTS, dtype=jnp.int32)[None, None, :, None]
    slot_total = local_experts * SLOTS
    match = match.astype(jnp.bfloat16).reshape(row_devices, slot_total, row_count)
    slot_shape = (row_devices, local_experts, SLOTS, model_width)
    one_shape = (row_devices, local_experts, SLOTS, 1)
    query_width = w_query.shape[1]
    key_width = key_weight.shape[1]
    qkv_raw = jnp.dot(normed_narrow, full_qkv, preferred_element_type=jnp.float32)
    query_raw = qkv_raw[:, :query_width].reshape(row_count, -1, HEAD_SIZE)
    key_unnormed = qkv_raw[:, query_width : query_width + key_width].reshape(
        row_count, -1, HEAD_SIZE
    )
    value_narrow = (
        qkv_raw[:, query_width + key_width :]
        .astype(jnp.bfloat16)
        .reshape(row_count, -1, HEAD_SIZE)
    )
    queries = head_prep(query_raw, q_gain, cosine, sine_table).astype(jnp.bfloat16)
    key_head_rows = head_prep(key_unnormed, k_gain, cosine, sine_table).astype(jnp.bfloat16)
    context, log_norm = attend_forward(queries, key_head_rows, value_narrow, visible)
    partial_attn = jnp.einsum("tc,dc->td", context, full_out, preferred_element_type=jnp.float32)
    hidden = own_share(tokens).astype(jnp.float32) + col_scatter(partial_attn.astype(jnp.bfloat16))
    ffn_low = rms_scale(hidden, ffn_gain).astype(jnp.bfloat16)
    ffn_all = lax.all_gather(ffn_low, everyone, axis=0, tiled=True)
    logits = jnp.dot(ffn_low, router, preferred_element_type=jnp.float32)
    gates_all = ring_gather(col_gather(dense_gates(logits, chosen_own.astype(jnp.float32))))
    gates_local = lax.dynamic_slice_in_dim(gates_all, first_local, local_experts, 1)
    gates_local = gates_local.reshape(row_devices, row_count, local_experts).transpose(0, 2, 1)
    gate_slots = gates_of_slots(match, gates_local).reshape(one_shape)
    grad_rows = rows_of_slots(match, cot_all).reshape(slot_shape)
    expert_rows = rows_of_slots(match, ffn_all).reshape(slot_shape)
    gated_out, grad_back, gate_grads, active, grad_gate_low, grad_up_low = expert_pass(
        expert_rows, grad_rows, gate_slots, w_gate, w_up, w_down
    )
    gate_tokens = gate_grads_to_tokens(
        match,
        gate_grads.reshape(row_devices, slot_total, 1),
        first_local.astype(jnp.int32).reshape(1),
        experts_all,
    )
    grad_back = grad_back.reshape(row_devices, slot_total, model_width)
    given = slots_to_tokens(match, grad_back, 1 - core, 2)
    taken = col_swap(given, 1)
    kept = slots_to_tokens(match, grad_back, core, 2)

    def pair_block(row):
        mine = lax.dynamic_slice_in_dim(kept, row * row_count, row_count, 0)
        theirs = lax.dynamic_slice_in_dim(taken, row * row_count, row_count, 0)
        gate_block = lax.dynamic_slice_in_dim(gate_tokens, row * row_count, row_count, 0)
        return [mine.astype(jnp.float32) + theirs.astype(jnp.float32), gate_block]

    pieces = 4 if local_experts % 4 == 0 else 1
    each = local_experts // pieces
    grad_inputs = (expert_rows, grad_rows, gate_slots, active, grad_gate_low, grad_up_low)

    def weight_grads(piece, earlier):
        return (
            lambda *operands: expert_weight_grads(
                piece * each, each, operands[:6], operands[6:]
            ),
            lambda filled: grad_inputs + tuple(earlier(filled)),
        )

    zero = jnp.zeros((1,), jnp.int32)
    out_filler = (
        lambda *operands: slots_to_tokens(*operands, zero, 1),
        (match, gated_out.reshape(row_devices, slot_total, model_width)),
    )
    weight_fillers = [
        weight_grads(piece, lambda filled, piece=piece: filled[-1 if piece > 1 else 0])
        for piece in range(1, pieces - 1)
    ]
    (half_sum, gate_sum), filled, unused = ring_scatter(
        pair_block,
        [jnp.bfloat16, jnp.bfloat16],
        [weight_grads(0, lambda filled: ()), out_filler] + weight_fillers,
    )
    out_tokens = filled[1]
    weights_so_far = filled[pieces - 1] if pieces > 2 else filled[0]
    for bit in reversed(col_bits()[1:]):
        keep, give = split_by_bit(half_sum, bit)
        half_sum = keep + col_swap(give.astype(jnp.bfloat16), bit).astype(jnp.float32)
    gate_sums = col_scatter(gate_sum.astype(jnp.bfloat16))
    keep, give = split_by_bit(half_sum, 1)
    across = col_swap(give.astype(jnp.bfloat16), 1).astype(jnp.float32)
    back_sum = jnp.where(
        col_at % 2 == 0,
        jnp.concatenate([keep, across], axis=1),
        jnp.concatenate([across, keep], axis=1),
    )
    mixture = lax.psum_scatter(out_tokens, everyone, scatter_dimension=0, tiled=True).astype(
        jnp.float32
    )
    grad_out = own_share(cotangent).astype(jnp.float32)
    unused, gate_pullback = jax.vjp(
        lambda raw_logits: dense_gates(raw_logits, chosen_own.astype(jnp.float32)), logits
    )
    grad_logits = gate_pullback(gate_sums)[0].astype(jnp.bfloat16)
    router_term = jnp.einsum("td,te->ed", ffn_low, grad_logits, preferred_element_type=jnp.float32)
    grad_ffn_normed = back_sum + jnp.einsum(
        "te,de->td", grad_logits, router, preferred_element_type=jnp.float32
    )
    unused, ffn_pullback = jax.vjp(rms_scale, hidden, ffn_gain)
    grad_hidden_norm, ffn_gain_term = ffn_pullback(grad_ffn_normed)
    grad_hidden = grad_out + grad_hidden_norm
    grad_hidden_low = col_gather(grad_hidden.astype(jnp.bfloat16))
    out_term = jnp.einsum("td,tc->dc", grad_hidden_low, context, preferred_element_type=jnp.float32)
    out_term = out_term.astype(jnp.bfloat16)

    extent = model_width // row_devices

    out_fillers = [
        (
            lambda rows, weights: jnp.einsum(
                "td,dc->tc", rows, weights, preferred_element_type=jnp.float32
            ).astype(jnp.bfloat16),
            (grad_hidden_low, full_out),
        ),
        (
            attend_backward,
            lambda filled: (
                queries, key_head_rows, value_narrow, visible, log_norm, context, filled[0]
            ),
        ),
    ]
    router_blocks = router_term.reshape(experts_all, row_devices, extent).transpose(1, 0, 2)
    router_blocks = router_blocks.astype(jnp.bfloat16)

    def out_blocks(row):
        return [
            lax.dynamic_slice_in_dim(out_term, row * extent, extent, 0),
            lax.dynamic_index_in_dim(router_blocks, row, 0, keepdims=False),
        ]

    (out_sums, router_sums), filled, unused = ring_scatter(
        out_blocks, [jnp.bfloat16, jnp.bfloat16], out_fillers
    )
    grad_queries, key_gradients, value_gradients = filled[1]
    unused, query_pullback = jax.vjp(
        lambda raw_heads, scaling: head_prep(raw_heads, scaling, cosine, sine_table),
        query_raw,
        q_gain,
    )
    grad_query_raw, q_gain_term = query_pullback(grad_queries)
    unused, key_reverse_map = jax.vjp(
        lambda raw_heads, scaling: head_prep(raw_heads, scaling, cosine, sine_table),
        key_unnormed,
        k_gain,
    )
    key_gradient_unnormed, k_gain_term = key_reverse_map(key_gradients)
    grad_qkv_low = jnp.concatenate(
        [
            grad_query_raw.reshape(row_count, query_width).astype(jnp.bfloat16),
            key_gradient_unnormed.reshape(row_count, key_width).astype(jnp.bfloat16),
            value_gradients.reshape(row_count, key_width).astype(jnp.bfloat16),
        ],
        axis=1,
    )
    qkv_term = jnp.einsum(
        "td,tc->dc", normed_narrow, grad_qkv_low, preferred_element_type=jnp.float32
    )
    partial_grad_normed = jnp.einsum(
        "tc,dc->td", grad_qkv_low, full_qkv, preferred_element_type=jnp.float32
    )
    unused, attn_pullback = jax.vjp(rms_scale, tokens_wide, attn_gain)
    attn_gain_term = attn_pullback(partial_grad_normed)[1]

    extent = model_width // row_devices
    head_share = HEAD_SIZE // row_devices

    def by_rows(gain_term):
        pieces = gain_term.reshape(row_devices, 1, -1)
        return jnp.pad(pieces, ((0, 0), (0, 0), (0, extent - pieces.shape[2])))

    gain_terms = jnp.concatenate(
        [
            by_rows(ffn_gain_term),
            by_rows(attn_gain_term),
            by_rows(q_gain_term),
            by_rows(k_gain_term),
            jnp.zeros((row_devices, 4, extent), jnp.float32),
        ],
        axis=1,
    )
    qkv_term = qkv_term.astype(jnp.bfloat16)

    def last_blocks(row):
        return [
            lax.dynamic_slice_in_dim(qkv_term, row * extent, extent, 0),
            lax.dynamic_index_in_dim(gain_terms, row, 0, keepdims=False),
        ]

    def finish(low_rows, summed_rows):
        return col_gather((low_rows + summed_rows).astype(jnp.bfloat16))

    last_weights = weight_grads(pieces - 1, lambda filled: weights_so_far)
    (qkv_sums, gain_sums), filled, marks = ring_scatter(
        last_blocks,
        [jnp.bfloat16, jnp.float32],
        [None, None, (finish, (hidden, mixture)), last_weights if pieces > 1 else None],
    )
    grad_w_gate, grad_w_up, grad_w_down = filled[3] if pieces > 1 else weights_so_far
    partial_low, unused = lax.optimization_barrier(
        (partial_grad_normed.astype(jnp.bfloat16), marks[0])
    )
    block_out = filled[2]
    gain_sums = col_sum(gain_sums)
    router_sums = col_sum(router_sums)
    grad_normed = col_gather(
        col_scatter(partial_low).astype(jnp.bfloat16)
    ).astype(jnp.float32)
    grad_tokens = grad_hidden_low.astype(jnp.float32) + attn_pullback(grad_normed)[0]
    grad_w_query = qkv_sums[:, :query_width]
    grad_w_key = qkv_sums[:, query_width : query_width + key_width]
    grad_w_value = qkv_sums[:, query_width + key_width :]
    return (
        block_out,
        grad_tokens,
        gain_sums[1],
        grad_w_query,
        grad_w_key,
        grad_w_value,
        out_sums,
        gain_sums[2, :head_share],
        gain_sums[3, :head_share],
        gain_sums[0],
        router_sums.T,
        grad_w_gate,
        grad_w_up,
        grad_w_down,
    )


def solution(mesh):
    in_specs = (
        P("row", None),
        P("row", None),
        P("row", None),
        P(),
        P("row", "col"),
        P("row", "col"),
        P("row", "col"),
        P("row", "col"),
        P(),
        P(),
        P(),
        P(),
        P("row", "col", None),
        P("row", "col", None),
        P("row", "col", None),
        P("row", None),
    )
    out_specs = (
        P("row", None),
        P("row", None),
        P("row"),
        P("row", "col"),
        P("row", "col"),
        P("row", "col"),
        P("row", "col"),
        P("row"),
        P("row"),
        P("row"),
        P("row", None),
        P("row", "col", None),
        P("row", "col", None),
        P("row", "col", None),
    )
    return jax.shard_map(shards, mesh=mesh, in_specs=in_specs, out_specs=out_specs, check_vma=False)
```

```python
import math

import jax
import jax.numpy as jnp
from jax import lax
from jax.experimental import pallas as pl
from jax.experimental.pallas import tpu as pltpu
from jax.sharding import PartitionSpec as P

HEAD_SIZE = 128
TOPK = 8
CAP = 36
CHUNK = 8
SLOTS = -(-CAP // 16) * 16


epsilon = 1e-06
rope_base = 1000000.0
masked_score = -1e30


def rms_scale(values, scaling):
    return values * lax.rsqrt(jnp.mean(values * values, axis=-1, keepdims=True) + epsilon) * scaling


def rope_tables(documents):
    length = documents.shape[0]
    earlier = jnp.sum((documents[None, :] < documents[:, None]).astype(jnp.int32), axis=1)
    position = (jnp.arange(length, dtype=jnp.int32) - earlier).astype(jnp.float32)
    half_width = HEAD_SIZE // 2
    exponent = jnp.arange(half_width, dtype=jnp.float32) * (-2.0 / HEAD_SIZE)
    frequency = jnp.power(jnp.float32(rope_base), exponent)
    angles = position[:, None] * frequency[None, :]
    return (jnp.cos(angles), jnp.sin(angles))


def visible_mask(documents):
    length = documents.shape[0]
    positions_in = jnp.arange(length, dtype=jnp.int32)
    return (documents[:, None] == documents[None, :]) & (
        positions_in[None, :] <= positions_in[:, None]
    )


def head_prep(raw_heads, scaling, cosine, sine_table):
    normed = rms_scale(raw_heads, scaling)
    half_width = raw_heads.shape[-1] // 2
    front_half = normed[..., :half_width]
    back_half = normed[..., half_width:]
    cos_rows = cosine[:, None, :]
    sin_rows = sine_table[:, None, :]
    return jnp.concatenate(
        [
            front_half * cos_rows - back_half * sin_rows,
            back_half * cos_rows + front_half * sin_rows,
        ],
        axis=-1,
    )


def dense_gates(logits, chosen):
    picked = jax.nn.softmax(logits, axis=-1) * chosen
    return picked / jnp.sum(picked, axis=-1, keepdims=True)


def chosen_experts(routes, expert_ids):
    hits = [(routes[:, k : k + 1] == expert_ids[None, :]) for k in range(TOPK)]
    found = hits[0]
    for hit in hits[1:]:
        found = found | hit
    return found


def attend_forward(queries, key_head_rows, value_heads, visible):
    row_count, head_count, head_width = queries.shape
    group_count = key_head_rows.shape[1]
    grouped = queries.reshape(row_count, group_count, head_count // group_count, head_width)
    scores = jnp.einsum(
        "tgrh,ugh->grtu", grouped, key_head_rows, preferred_element_type=jnp.float32
    ) * head_width ** (-0.5)
    scores = jnp.where(visible[None, None], scores, masked_score)
    row_peak = jnp.max(scores, axis=-1, keepdims=True)
    log_norm = row_peak + jnp.log(jnp.sum(jnp.exp(scores - row_peak), axis=-1, keepdims=True))
    attn_weights = jnp.exp(scores - log_norm).astype(jnp.bfloat16)
    context = jnp.einsum(
        "grtu,ugh->tgrh", attn_weights, value_heads, preferred_element_type=jnp.float32
    )
    return (context.reshape(row_count, head_count * head_width).astype(jnp.bfloat16), log_norm)


def attend_backward(queries, key_head_rows, value_heads, visible, log_norm, context, grad_context):
    row_count, head_count, head_width = queries.shape
    group_count = key_head_rows.shape[1]
    repeat = head_count // group_count
    factor = head_width ** (-0.5)
    grouped = queries.reshape(row_count, group_count, repeat, head_width)
    scores = (
        jnp.einsum("tgrh,ugh->grtu", grouped, key_head_rows, preferred_element_type=jnp.float32)
        * factor
    )
    scores = jnp.where(visible[None, None], scores, masked_score)
    weights_wide = jnp.exp(scores - log_norm)
    weights_low = weights_wide.astype(jnp.bfloat16)
    gradient_by_group = grad_context.reshape(row_count, group_count, repeat, head_width)
    context_by_group = context.reshape(row_count, group_count, repeat, head_width)
    grad_weights = jnp.einsum(
        "tgrh,ugh->grtu", gradient_by_group, value_heads, preferred_element_type=jnp.float32
    )
    row_product_sum = jnp.einsum(
        "xjds,xjds->jdx",
        gradient_by_group.astype(jnp.float32),
        context_by_group.astype(jnp.float32),
    )
    grad_scores = (weights_wide * (grad_weights - row_product_sum[..., None]) * factor).astype(
        jnp.bfloat16
    )
    grad_queries = jnp.einsum(
        "grtu,ugh->tgrh", grad_scores, key_head_rows, preferred_element_type=jnp.float32
    )
    key_gradients = jnp.einsum(
        "grtu,tgrh->ugh", grad_scores, grouped, preferred_element_type=jnp.float32
    )
    value_gradients = jnp.einsum(
        "grtu,tgrh->ugh", weights_low, gradient_by_group, preferred_element_type=jnp.float32
    )
    return (grad_queries.reshape(row_count, head_count, head_width), key_gradients, value_gradients)


def ring_order(count):
    evens = list(range(0, count, 2))
    odds = list(range(1, count, 2))
    return evens + odds[::-1]


def ring_links(count):
    order = ring_order(count)
    ahead = [(order[i], order[(i + 1) % count]) for i in range(count)]
    return ahead, [(there, here) for here, there in ahead]


def ring_neighbour(distance):
    count = lax.axis_size("row")
    order = ring_order(count)
    places = [order[(order.index(row) + distance) % count] for row in range(count)]
    return jnp.asarray(places, jnp.int32)[lax.axis_index("row")]


def ring_gather_pieces(shards, alongside=()):
    count = lax.axis_size("row")
    ahead, behind = ring_links(count)
    pieces = [[(lax.axis_index("row"), 0, shard)] for shard in shards]
    forward = backward = list(shards)
    made = list(alongside)
    for step in range(1, count // 2):
        forward = [lax.ppermute(piece, "row", ahead) for piece in forward]
        backward = [lax.ppermute(piece, "row", behind) for piece in backward]
        if step <= len(made):
            forward, backward, made[step - 1] = lax.optimization_barrier(
                (forward, backward, made[step - 1])
            )
        else:
            forward, backward = lax.optimization_barrier((forward, backward))
        for found, one, other in zip(pieces, forward, backward):
            found.append((ring_neighbour(-step), 0, one))
            found.append((ring_neighbour(step), 0, other))
    far = ring_neighbour(count // 2)
    for found, one, other in zip(pieces, forward, backward):
        middle = one.shape[0] // 2
        found.append((far, 0, lax.ppermute(one[:middle], "row", ahead)))
        found.append((far, middle, lax.ppermute(other[middle:], "row", behind)))
    return pieces, made


def assembled(pieces, extent):
    whole = jnp.zeros((lax.axis_size("row") * extent, pieces[0][2].shape[1]), pieces[0][2].dtype)
    for origin, offset, piece in pieces:
        whole = lax.dynamic_update_slice(whole, piece, (origin * extent + offset, 0))
    return whole


def ring_gather(shard):
    return assembled(ring_gather_pieces([shard])[0][0], shard.shape[0])


def ring_scatter(blocks_of, wires, fillers=()):
    count = lax.axis_size("row")
    ahead, behind = ring_links(count)
    half = count // 2
    filled = []
    marks = []

    def wide(arrays):
        return [array.astype(jnp.float32) for array in arrays]

    def hop(to_ahead, to_behind):
        step = len(filled)
        to_ahead = [array.astype(wire) for array, wire in zip(to_ahead, wires)]
        to_behind = [array.astype(wire) for array, wire in zip(to_behind, wires)]
        filler = fillers[step] if step < len(fillers) else None
        if filler is not None:
            work, operands = filler
            operands = operands(filled) if callable(operands) else operands
            operands, to_ahead, to_behind = lax.optimization_barrier(
                (operands, to_ahead, to_behind)
            )
        forward = [lax.ppermute(array, "row", ahead) for array in to_ahead]
        backward = [lax.ppermute(array, "row", behind) for array in to_behind]
        marks.append(forward[-1])
        if filler is not None:
            forward, backward, made = lax.optimization_barrier(
                (forward, backward, work(*operands))
            )
        else:
            forward, backward = lax.optimization_barrier((forward, backward))
            made = None
        filled.append(made)
        return wide(forward), wide(backward)

    far = blocks_of(ring_neighbour(half))
    middles = [array.shape[0] // 2 for array in far]
    forward, backward = hop(
        [array[:middle] for array, middle in zip(far, middles)],
        [array[middle:] for array, middle in zip(far, middles)],
    )
    for distance in range(half - 1, -1, -1):
        to_ahead = wide(blocks_of(ring_neighbour(distance)))
        to_behind = wide(blocks_of(ring_neighbour(-distance)))
        if distance == half - 1:
            to_ahead = [
                jnp.concatenate([own[:middle] + came, own[middle:]], axis=0)
                for own, came, middle in zip(to_ahead, forward, middles)
            ]
            to_behind = [
                jnp.concatenate([own[:middle], own[middle:] + came], axis=0)
                for own, came, middle in zip(to_behind, backward, middles)
            ]
        else:
            to_ahead = [own + came for own, came in zip(to_ahead, forward)]
            to_behind = [own + came for own, came in zip(to_behind, backward)]
        if distance == 0:
            return [one + came for one, came in zip(to_ahead, backward)], filled, marks
        forward, backward = hop(to_ahead, to_behind)


def col_bits():
    count = lax.axis_size("col")
    return [1 << bit for bit in range(count.bit_length() - 1)]


def col_swap(values, bit):
    count = lax.axis_size("col")
    return lax.ppermute(values, "col", [(c, c ^ bit) for c in range(count)])


def split_by_bit(values, bit):
    half = values.shape[0] // 2
    mine = (lax.axis_index("col") // bit) % 2
    keep = lax.dynamic_slice_in_dim(values, mine * half, half, 0)
    give = lax.dynamic_slice_in_dim(values, (1 - mine) * half, half, 0)
    return keep, give


def col_scatter(values):
    count = lax.axis_size("col")
    blocks = values.reshape((count, -1) + values.shape[1:])
    low = blocks.reshape((count // 2, 2) + blocks.shape[1:])
    core = lax.axis_index("col") % 2
    keep = lax.dynamic_index_in_dim(low, core, 1, keepdims=False)
    give = lax.dynamic_index_in_dim(low, 1 - core, 1, keepdims=False)
    total = keep.astype(jnp.float32) + col_swap(give, 1).astype(jnp.float32)
    for bit in reversed(col_bits()[1:]):
        keep, give = split_by_bit(total, bit)
        total = keep + col_swap(give.astype(values.dtype), bit).astype(jnp.float32)
    return total[0]


def col_gather(share):
    count = lax.axis_size("col")
    whole = share[None]
    for bit in reversed(col_bits()):
        other = col_swap(whole, bit)
        mine = (lax.axis_index("col") // bit) % 2
        first = jnp.where(mine == 0, whole, other)
        second = jnp.where(mine == 0, other, whole)
        whole = jnp.stack([first, second], axis=0)
    axes = [len(col_bits()) - 1 - i for i in range(len(col_bits()))]
    whole = whole.reshape((2,) * len(col_bits()) + share.shape)
    whole = whole.transpose(axes + list(range(len(axes), whole.ndim)))
    return whole.reshape((count * share.shape[0],) + share.shape[1:])


def col_sum(values):
    for bit in col_bits():
        values = values + col_swap(values, bit)
    return values


def contract(left, right, left_axis, right_axis):
    return lax.dot_general(
        left,
        right,
        (((left_axis,), (right_axis,)), ((), ())),
        preferred_element_type=jnp.float32,
    )


def whole_block(shape, index_map):
    return pl.BlockSpec(shape, index_map)


def rows_of_slots(match, rows):
    sequences, slot_count, row_count = match.shape
    width = rows.shape[1]

    def kernel(match_ref, rows_ref, out_ref):
        out_ref[0] = contract(match_ref[0], rows_ref[...], 1, 0).astype(out_ref.dtype)

    return pl.pallas_call(
        kernel,
        grid=(sequences,),
        in_specs=[
            whole_block((1, slot_count, row_count), lambda s: (s, 0, 0)),
            whole_block((row_count, width), lambda s: (s, 0)),
        ],
        out_specs=whole_block((1, slot_count, width), lambda s: (s, 0, 0)),
        out_shape=jax.ShapeDtypeStruct((sequences, slot_count, width), rows.dtype),
        name="rows_of_slots",
    )(match, rows)


def gates_of_slots(match, gates):
    sequences, slot_count, row_count = match.shape
    experts = gates.shape[1]

    def kernel(match_ref, gates_ref, out_ref):
        wide = match_ref[0].astype(jnp.float32).reshape(experts, -1, row_count)
        picked = jnp.sum(wide * gates_ref[0][:, None, :], axis=-1, keepdims=True)
        out_ref[0] = picked.reshape(slot_count, 1)

    return pl.pallas_call(
        kernel,
        grid=(sequences,),
        in_specs=[
            whole_block((1, slot_count, row_count), lambda s: (s, 0, 0)),
            whole_block((1, experts, row_count), lambda s: (s, 0, 0)),
        ],
        out_specs=whole_block((1, slot_count, 1), lambda s: (s, 0, 0)),
        out_shape=jax.ShapeDtypeStruct((sequences, slot_count, 1), jnp.float32),
        name="gates_of_slots",
    )(match, gates)


def expert_pass(expert_rows, grad_rows, gate_slots, w_gate, w_up, w_down):
    sequences, experts, slots, width = expert_rows.shape
    hidden_units = w_gate.shape[1]
    chunk = math.gcd(sequences, CHUNK)
    rows = chunk * slots

    def kernel(x_ref, g_ref, gate_ref, wg_ref, wu_ref, wd_ref, out_ref, back_ref, gg_ref, act_ref, dg_ref, du_ref):
        x = x_ref[...].reshape(rows, width)
        gate = gate_ref[...].reshape(rows, 1)
        gate_pre = contract(x, wg_ref[0], 1, 1)
        up_pre = contract(x, wu_ref[0], 1, 1)
        sigmoid_gate = jax.nn.sigmoid(gate_pre)
        silu_gate = gate_pre * sigmoid_gate
        active = (silu_gate * up_pre).astype(jnp.bfloat16)
        act_ref[0] = active
        grad_wide = g_ref[...].reshape(rows, width).astype(jnp.float32)
        grad_expert = (gate * grad_wide).astype(jnp.bfloat16)
        grad_active = contract(grad_expert, wd_ref[0], 1, 1)
        grad_gate_low = (
            grad_active * up_pre * sigmoid_gate * (1.0 + gate_pre * (1.0 - sigmoid_gate))
        ).astype(jnp.bfloat16)
        grad_up_low = (grad_active * silu_gate).astype(jnp.bfloat16)
        dg_ref[0] = grad_gate_low
        du_ref[0] = grad_up_low
        back = contract(grad_gate_low, wg_ref[0], 1, 0) + contract(grad_up_low, wu_ref[0], 1, 0)
        back_ref[...] = back.astype(jnp.bfloat16).reshape(chunk, 1, slots, width)
        expert_out = contract(active, wd_ref[0], 1, 0)
        gg_ref[...] = jnp.sum(expert_out * grad_wide, axis=-1, keepdims=True).reshape(
            chunk, 1, slots, 1
        )
        out_ref[...] = (gate * expert_out).astype(jnp.bfloat16).reshape(chunk, 1, slots, width)

    row_spec = whole_block((chunk, 1, slots, width), lambda e, c: (c, e, 0, 0))
    one_spec = whole_block((chunk, 1, slots, 1), lambda e, c: (c, e, 0, 0))
    weight_spec = whole_block((1, hidden_units, width), lambda e, c: (e, 0, 0))
    hidden_spec = whole_block((1, rows, hidden_units), lambda e, c: (e, c, 0))
    row_shape = jax.ShapeDtypeStruct(expert_rows.shape, jnp.bfloat16)
    hidden_shape = jax.ShapeDtypeStruct((experts, sequences * slots, hidden_units), jnp.bfloat16)
    return pl.pallas_call(
        kernel,
        grid=(experts, sequences // chunk),
        in_specs=[row_spec, row_spec, one_spec, weight_spec, weight_spec, weight_spec],
        out_specs=[row_spec, row_spec, one_spec, hidden_spec, hidden_spec, hidden_spec],
        out_shape=[
            row_shape,
            row_shape,
            jax.ShapeDtypeStruct((sequences, experts, slots, 1), jnp.float32),
            hidden_shape,
            hidden_shape,
            hidden_shape,
        ],
        name="expert_pass",
    )(expert_rows, grad_rows, gate_slots, w_gate, w_up, w_down)


def expert_weight_grads(first, count, operands, earlier):
    sequences, experts, slots, width = operands[0].shape
    hidden_units = operands[3].shape[2]
    chunk = math.gcd(sequences, CHUNK)
    rows = chunk * slots

    def kernel(x_ref, g_ref, gate_ref, act_ref, dg_ref, du_ref, *rest):
        def put(out_ref, left, right):
            term = contract(left, right, 0, 0)
            if sequences == chunk:
                out_ref[0] = term
            else:
                out_ref[0] = term + jnp.where(pl.program_id(1) == 0, 0.0, out_ref[0])

        wg_ref, wu_ref, wd_ref = rest[-3:]
        x = x_ref[...].reshape(rows, width)
        put(wg_ref, dg_ref[0], x)
        put(wu_ref, du_ref[0], x)
        grad_expert = (
            gate_ref[...].reshape(rows, 1) * g_ref[...].reshape(rows, width).astype(jnp.float32)
        ).astype(jnp.bfloat16)
        put(wd_ref, act_ref[0], grad_expert)

    row_spec = whole_block((chunk, 1, slots, width), lambda e, c: (c, first + e, 0, 0))
    one_spec = whole_block((chunk, 1, slots, 1), lambda e, c: (c, first + e, 0, 0))
    weight_spec = whole_block((1, hidden_units, width), lambda e, c: (first + e, 0, 0))
    hidden_spec = whole_block((1, rows, hidden_units), lambda e, c: (first + e, c, 0))
    weight_shape = jax.ShapeDtypeStruct((experts, hidden_units, width), jnp.float32)
    return pl.pallas_call(
        kernel,
        grid=(count, sequences // chunk),
        in_specs=[row_spec, row_spec, one_spec, hidden_spec, hidden_spec, hidden_spec]
        + [pl.BlockSpec(memory_space=pl.ANY)] * len(earlier),
        out_specs=[weight_spec, weight_spec, weight_spec],
        out_shape=[weight_shape, weight_shape, weight_shape],
        input_output_aliases={6 + i: i for i in range(len(earlier))},
        name="expert_weight_grads",
    )(*operands, *earlier)


def slots_to_tokens(match, slot_rows, part, parts):
    sequences, slot_count, row_count = match.shape
    width = slot_rows.shape[2] // parts

    def kernel(part_ref, match_ref, rows_ref, out_ref):
        out_ref[...] = contract(match_ref[0], rows_ref[0], 0, 0).astype(jnp.bfloat16)

    return pl.pallas_call(
        kernel,
        grid_spec=pltpu.PrefetchScalarGridSpec(
            num_scalar_prefetch=1,
            grid=(sequences,),
            in_specs=[
                whole_block((1, slot_count, row_count), lambda s, part: (s, 0, 0)),
                whole_block((1, slot_count, width), lambda s, part: (s, 0, part[0])),
            ],
            out_specs=whole_block((row_count, width), lambda s, part: (s, 0)),
        ),
        out_shape=jax.ShapeDtypeStruct((sequences * row_count, width), jnp.bfloat16),
        name="slots_to_tokens",
    )(part, match, slot_rows)


def gate_grads_to_tokens(match, gate_grads, first_expert, experts_all):
    sequences, slot_count, row_count = match.shape

    def kernel(first_ref, match_ref, gate_ref, out_ref):
        expert_of_slot = first_ref[0] + lax.broadcasted_iota(
            jnp.int32, (slot_count // SLOTS, SLOTS, experts_all), 0
        ).reshape(slot_count, experts_all)
        column = lax.broadcasted_iota(jnp.int32, (slot_count, experts_all), 1)
        placed = jnp.where(column == expert_of_slot, gate_ref[0], 0.0).astype(jnp.bfloat16)
        out_ref[...] = contract(match_ref[0], placed, 0, 0).astype(jnp.bfloat16)

    return pl.pallas_call(
        kernel,
        grid_spec=pltpu.PrefetchScalarGridSpec(
            num_scalar_prefetch=1,
            grid=(sequences,),
            in_specs=[
                whole_block((1, slot_count, row_count), lambda s, first: (s, 0, 0)),
                whole_block((1, slot_count, 1), lambda s, first: (s, 0, 0)),
            ],
            out_specs=whole_block((row_count, experts_all), lambda s, first: (s, 0)),
        ),
        out_shape=jax.ShapeDtypeStruct((sequences * row_count, experts_all), jnp.bfloat16),
        name="gate_grads_to_tokens",
    )(first_expert, match, gate_grads)


def shards(
    tokens,
    doc_ids,
    routes,
    attn_gain,
    w_query,
    key_weight,
    value_weight,
    w_out,
    q_gain,
    k_gain,
    ffn_gain,
    router,
    w_gate,
    w_up,
    w_down,
    cotangent,
):
    row_count, model_width = tokens.shape
    row_devices = lax.axis_size("row")
    col_devices = lax.axis_size("col")
    row_at = lax.axis_index("row")
    col_at = lax.axis_index("col")
    experts_all = router.shape[1]
    local_experts = w_gate.shape[0]
    token_total = row_count * row_devices
    share = row_count // col_devices
    documents = doc_ids[0]
    everyone = ("row", "col")

    def own_share(rows):
        return lax.dynamic_slice_in_dim(rows, col_at * share, share, 0)

    qkv_width = w_query.shape[1] + key_weight.shape[1] + value_weight.shape[1]
    expert_ids = jnp.arange(experts_all, dtype=jnp.int32)
    chosen_row = chosen_experts(routes, expert_ids).astype(jnp.bfloat16)
    chosen_own = own_share(chosen_row)
    tokens_wide = tokens.astype(jnp.float32)
    normed_narrow = rms_scale(tokens_wide, attn_gain).astype(jnp.bfloat16)
    (qkv_pieces, chosen_pieces), made = ring_gather_pieces(
        [jnp.concatenate([w_query, key_weight, value_weight], axis=1), chosen_row],
        [rope_tables(documents), (normed_narrow, visible_mask(documents))],
    )
    (cosine, sine_table), (normed_narrow, visible) = made
    full_qkv = assembled(qkv_pieces, w_query.shape[0])
    chosen_all = assembled(chosen_pieces, row_count)
    w_out_after, unused = lax.optimization_barrier((w_out, qkv_pieces[-1][2]))
    out_pieces = ring_gather_pieces([w_out_after])[0][0]
    full_out = assembled(out_pieces, w_out.shape[0])
    core = (col_at % 2).astype(jnp.int32).reshape(1)
    cot_share, unused = lax.optimization_barrier((own_share(cotangent), out_pieces[-4][2]))
    cot_all = lax.all_gather(cot_share, everyone, axis=0, tiled=True)

    first_local = row_at * local_experts
    chosen_local = lax.dynamic_slice_in_dim(chosen_all, first_local, local_experts, 1).reshape(
        row_devices, row_count, local_experts
    )
    positions = jnp.arange(row_count, dtype=jnp.int32)
    earlier = (positions[None, :] < positions[:, None]).astype(jnp.bfloat16)
    rank = jnp.einsum("tu,sue->set", earlier, chosen_local, preferred_element_type=jnp.float32)
    rank = jnp.where(chosen_local.transpose(0, 2, 1) > 0, rank.astype(jnp.int32), SLOTS)
    match = rank[:, :, None, :] == jnp.arange(SLOTS, dtype=jnp.int32)[None, None, :, None]
    slot_total = local_experts * SLOTS
    match = match.astype(jnp.bfloat16).reshape(row_devices, slot_total, row_count)
    slot_shape = (row_devices, local_experts, SLOTS, model_width)
    one_shape = (row_devices, local_experts, SLOTS, 1)
    query_width = w_query.shape[1]
    key_width = key_weight.shape[1]
    qkv_raw = jnp.dot(normed_narrow, full_qkv, preferred_element_type=jnp.float32)
    query_raw = qkv_raw[:, :query_width].reshape(row_count, -1, HEAD_SIZE)
    key_unnormed = qkv_raw[:, query_width : query_width + key_width].reshape(
        row_count, -1, HEAD_SIZE
    )
    value_narrow = (
        qkv_raw[:, query_width + key_width :]
        .astype(jnp.bfloat16)
        .reshape(row_count, -1, HEAD_SIZE)
    )
    queries = head_prep(query_raw, q_gain, cosine, sine_table).astype(jnp.bfloat16)
    key_head_rows = head_prep(key_unnormed, k_gain, cosine, sine_table).astype(jnp.bfloat16)
    context, log_norm = attend_forward(queries, key_head_rows, value_narrow, visible)
    partial_attn = jnp.einsum("tc,dc->td", context, full_out, preferred_element_type=jnp.float32)
    hidden = own_share(tokens).astype(jnp.float32) + col_scatter(partial_attn.astype(jnp.bfloat16))
    ffn_low = rms_scale(hidden, ffn_gain).astype(jnp.bfloat16)
    ffn_all = lax.all_gather(ffn_low, everyone, axis=0, tiled=True)
    logits = jnp.dot(ffn_low, router, preferred_element_type=jnp.float32)
    gates_all = ring_gather(col_gather(dense_gates(logits, chosen_own.astype(jnp.float32))))
    gates_local = lax.dynamic_slice_in_dim(gates_all, first_local, local_experts, 1)
    gates_local = gates_local.reshape(row_devices, row_count, local_experts).transpose(0, 2, 1)
    gate_slots = gates_of_slots(match, gates_local).reshape(one_shape)
    grad_rows = rows_of_slots(match, cot_all).reshape(slot_shape)
    expert_rows = rows_of_slots(match, ffn_all).reshape(slot_shape)
    gated_out, grad_back, gate_grads, active, grad_gate_low, grad_up_low = expert_pass(
        expert_rows, grad_rows, gate_slots, w_gate, w_up, w_down
    )
    gate_tokens = gate_grads_to_tokens(
        match,
        gate_grads.reshape(row_devices, slot_total, 1),
        first_local.astype(jnp.int32).reshape(1),
        experts_all,
    )
    grad_back = grad_back.reshape(row_devices, slot_total, model_width)
    given = slots_to_tokens(match, grad_back, 1 - core, 2)
    taken = col_swap(given, 1)
    kept = slots_to_tokens(match, grad_back, core, 2)

    def pair_block(row):
        mine = lax.dynamic_slice_in_dim(kept, row * row_count, row_count, 0)
        theirs = lax.dynamic_slice_in_dim(taken, row * row_count, row_count, 0)
        gate_block = lax.dynamic_slice_in_dim(gate_tokens, row * row_count, row_count, 0)
        return [mine.astype(jnp.float32) + theirs.astype(jnp.float32), gate_block]

    pieces = 4 if local_experts % 4 == 0 else 1
    each = local_experts // pieces
    grad_inputs = (expert_rows, grad_rows, gate_slots, active, grad_gate_low, grad_up_low)

    def weight_grads(piece, earlier):
        return (
            lambda *operands: expert_weight_grads(
                piece * each, each, operands[:6], operands[6:]
            ),
            lambda filled: grad_inputs + tuple(earlier(filled)),
        )

    zero = jnp.zeros((1,), jnp.int32)
    out_filler = (
        lambda *operands: slots_to_tokens(*operands, zero, 1),
        (match, gated_out.reshape(row_devices, slot_total, model_width)),
    )
    weight_fillers = [
        weight_grads(piece, lambda filled, piece=piece: filled[-1 if piece > 1 else 0])
        for piece in range(1, pieces - 1)
    ]
    (half_sum, gate_sum), filled, unused = ring_scatter(
        pair_block,
        [jnp.bfloat16, jnp.bfloat16],
        [weight_grads(0, lambda filled: ()), out_filler] + weight_fillers,
    )
    out_tokens = filled[1]
    weights_so_far = filled[pieces - 1] if pieces > 2 else filled[0]
    for bit in reversed(col_bits()[1:]):
        keep, give = split_by_bit(half_sum, bit)
        half_sum = keep + col_swap(give.astype(jnp.bfloat16), bit).astype(jnp.float32)
    gate_sums = col_scatter(gate_sum.astype(jnp.bfloat16))
    keep, give = split_by_bit(half_sum, 1)
    across = col_swap(give.astype(jnp.bfloat16), 1).astype(jnp.float32)
    back_sum = jnp.where(
        col_at % 2 == 0,
        jnp.concatenate([keep, across], axis=1),
        jnp.concatenate([across, keep], axis=1),
    )
    mixture = lax.psum_scatter(out_tokens, everyone, scatter_dimension=0, tiled=True).astype(
        jnp.float32
    )
    grad_out = own_share(cotangent).astype(jnp.float32)
    unused, gate_pullback = jax.vjp(
        lambda raw_logits: dense_gates(raw_logits, chosen_own.astype(jnp.float32)), logits
    )
    grad_logits = gate_pullback(gate_sums)[0].astype(jnp.bfloat16)
    router_term = jnp.einsum("td,te->ed", ffn_low, grad_logits, preferred_element_type=jnp.float32)
    grad_ffn_normed = back_sum + jnp.einsum(
        "te,de->td", grad_logits, router, preferred_element_type=jnp.float32
    )
    unused, ffn_pullback = jax.vjp(rms_scale, hidden, ffn_gain)
    grad_hidden_norm, ffn_gain_term = ffn_pullback(grad_ffn_normed)
    grad_hidden = grad_out + grad_hidden_norm
    grad_hidden_low = col_gather(grad_hidden.astype(jnp.bfloat16))
    out_term = jnp.einsum("td,tc->dc", grad_hidden_low, context, preferred_element_type=jnp.float32)
    out_term = out_term.astype(jnp.bfloat16)

    extent = model_width // row_devices

    out_fillers = [
        (
            lambda rows, weights: jnp.einsum(
                "td,dc->tc", rows, weights, preferred_element_type=jnp.float32
            ).astype(jnp.bfloat16),
            (grad_hidden_low, full_out),
        ),
        (
            attend_backward,
            lambda filled: (
                queries, key_head_rows, value_narrow, visible, log_norm, context, filled[0]
            ),
        ),
    ]
    router_blocks = router_term.reshape(experts_all, row_devices, extent).transpose(1, 0, 2)
    router_blocks = router_blocks.astype(jnp.bfloat16)

    def out_blocks(row):
        return [
            lax.dynamic_slice_in_dim(out_term, row * extent, extent, 0),
            lax.dynamic_index_in_dim(router_blocks, row, 0, keepdims=False),
        ]

    (out_sums, router_sums), filled, unused = ring_scatter(
        out_blocks, [jnp.bfloat16, jnp.bfloat16], out_fillers
    )
    grad_queries, key_gradients, value_gradients = filled[1]
    unused, query_pullback = jax.vjp(
        lambda raw_heads, scaling: head_prep(raw_heads, scaling, cosine, sine_table),
        query_raw,
        q_gain,
    )
    grad_query_raw, q_gain_term = query_pullback(grad_queries)
    unused, key_reverse_map = jax.vjp(
        lambda raw_heads, scaling: head_prep(raw_heads, scaling, cosine, sine_table),
        key_unnormed,
        k_gain,
    )
    key_gradient_unnormed, k_gain_term = key_reverse_map(key_gradients)
    grad_qkv_low = jnp.concatenate(
        [
            grad_query_raw.reshape(row_count, query_width).astype(jnp.bfloat16),
            key_gradient_unnormed.reshape(row_count, key_width).astype(jnp.bfloat16),
            value_gradients.reshape(row_count, key_width).astype(jnp.bfloat16),
        ],
        axis=1,
    )
    qkv_term = jnp.einsum(
        "td,tc->dc", normed_narrow, grad_qkv_low, preferred_element_type=jnp.float32
    )
    partial_grad_normed = jnp.einsum(
        "tc,dc->td", grad_qkv_low, full_qkv, preferred_element_type=jnp.float32
    )
    unused, attn_pullback = jax.vjp(rms_scale, tokens_wide, attn_gain)
    attn_gain_term = attn_pullback(partial_grad_normed)[1]

    extent = model_width // row_devices
    head_share = HEAD_SIZE // row_devices

    def by_rows(gain_term):
        pieces = gain_term.reshape(row_devices, 1, -1)
        return jnp.pad(pieces, ((0, 0), (0, 0), (0, extent - pieces.shape[2])))

    gain_terms = jnp.concatenate(
        [
            by_rows(ffn_gain_term),
            by_rows(attn_gain_term),
            by_rows(q_gain_term),
            by_rows(k_gain_term),
            jnp.zeros((row_devices, 4, extent), jnp.float32),
        ],
        axis=1,
    )
    qkv_term = qkv_term.astype(jnp.bfloat16)

    def last_blocks(row):
        return [
            lax.dynamic_slice_in_dim(qkv_term, row * extent, extent, 0),
            lax.dynamic_index_in_dim(gain_terms, row, 0, keepdims=False),
        ]

    def finish(low_rows, summed_rows):
        return col_gather((low_rows + summed_rows).astype(jnp.bfloat16))

    last_weights = weight_grads(pieces - 1, lambda filled: weights_so_far)
    (qkv_sums, gain_sums), filled, marks = ring_scatter(
        last_blocks,
        [jnp.bfloat16, jnp.float32],
        [None, None, (finish, (hidden, mixture)), last_weights if pieces > 1 else None],
    )
    grad_w_gate, grad_w_up, grad_w_down = filled[3] if pieces > 1 else weights_so_far
    partial_low, unused = lax.optimization_barrier(
        (partial_grad_normed.astype(jnp.bfloat16), marks[0])
    )
    block_out = filled[2]
    gain_sums = col_sum(gain_sums)
    router_sums = col_sum(router_sums)
    grad_normed = col_gather(
        col_scatter(partial_low).astype(jnp.bfloat16)
    ).astype(jnp.float32)
    grad_tokens = grad_hidden_low.astype(jnp.float32) + attn_pullback(grad_normed)[0]
    grad_w_query = qkv_sums[:, :query_width]
    grad_w_key = qkv_sums[:, query_width : query_width + key_width]
    grad_w_value = qkv_sums[:, query_width + key_width :]
    return (
        block_out,
        grad_tokens,
        gain_sums[1],
        grad_w_query,
        grad_w_key,
        grad_w_value,
        out_sums,
        gain_sums[2, :head_share],
        gain_sums[3, :head_share],
        gain_sums[0],
        router_sums.T,
        grad_w_gate,
        grad_w_up,
        grad_w_down,
    )


def solution(mesh):
    in_specs = (
        P("row", None),
        P("row", None),
        P("row", None),
        P(),
        P("row", "col"),
        P("row", "col"),
        P("row", "col"),
        P("row", "col"),
        P(),
        P(),
        P(),
        P(),
        P("row", "col", None),
        P("row", "col", None),
        P("row", "col", None),
        P("row", None),
    )
    out_specs = (
        P("row", None),
        P("row", None),
        P("row"),
        P("row", "col"),
        P("row", "col"),
        P("row", "col"),
        P("row", "col"),
        P("row"),
        P("row"),
        P("row"),
        P("row", None),
        P("row", "col", None),
        P("row", "col", None),
        P("row", "col", None),
    )
    return jax.shard_map(shards, mesh=mesh, in_specs=in_specs, out_specs=out_specs, check_vma=False)
```
